128 devices in a mesh: head: 4 (over z), seq: 32 (over y, x, core).
Axes of the slice: x: 4, y: 4, z: 4, core: 2. Of those that a mesh axis runs over, the one named last changes fastest.
Arguments:
- queries: bfloat16 [16384, 6144], P('seq', 'head'), may hold values from -60 to 60
- keys: bfloat16 [16384, 6144], P('seq', 'head'), may hold values from -6 to 6
- values: bfloat16 [16384, 6144], P('seq', 'head'), may hold values from -6 to 6
- cluster_ids: int32 [4, 16384, 1], P('head', 'seq'), may hold values from 0 to 255, as said below
- w_out: bfloat16 [6144, 6144], P('head'), may hold values from -0.078125 to 0.078125
Outputs:
- projected: bfloat16 [16384, 6144], P('seq', 'head')
The draws below stay inside these ranges and needn't reach their ends.
Inputs may be any that keep to these rules, and one draw needn't show every extreme that they name: `cluster_ids`: cluster c is owned by index c // (256 / 32) of seq. Among the 512 tokens of one index of seq, in one head group, at most 4 name the same cluster and at most 24 name clusters of the same owner; both bounds are reached in every such block.
All inputs are finite; a program needn't handle non-finite values.
Results may differ from the reference program's by a relative error of at most 0.009.
Values may be sent and summed in bfloat16 or wider, within the bound.
A program may use at most 128 MiB of HBM per device.

```python
import math
import jax
import jax.numpy as jnp
from jax import lax

D = 6144
HEADS = 48
HD = 128
NCLUST = 256
TOK_DEV = 512
CAP = 4
GROUPS = 4
TOKENS = 16384
N_HEAD = 4
N_SEQ = 32


def draw_queries(key, part):
    drawn = jnp.clip(jax.random.normal(jax.random.fold_in(key, 1), (TOKENS, HEADS * HD), jnp.float32), -6.0, 6.0)
    return drawn.astype(jnp.bfloat16)


def draw_keys(key, part):
    drawn = jnp.clip(jax.random.normal(jax.random.fold_in(key, 3), (TOKENS, HEADS * HD), jnp.float32), -6.0, 6.0)
    return drawn.astype(jnp.bfloat16)


def draw_cluster_ids(key, part):
    mean_rows = TOK_DEV // N_SEQ
    half_rows = mean_rows // 2
    local_clusters = NCLUST // N_SEQ
    owner_slots = local_clusters * CAP
    slot_order = jnp.arange(owner_slots, dtype=jnp.int32)
    owner_order = jnp.arange(N_SEQ, dtype=jnp.int32)
    flat_order = jnp.arange(N_SEQ * owner_slots, dtype=jnp.int32)

    def one_group(group_key):
        owner_perm = jax.random.permutation(jax.random.fold_in(group_key, 1), N_SEQ).astype(jnp.int32)

        def one_block(block_key):
            shifts = jax.random.randint(jax.random.fold_in(block_key, 1), (N_SEQ // 2,), 0, half_rows + 1).astype(jnp.int32)
            shifts = shifts.at[0].set(half_rows)
            paired = jnp.stack([mean_rows + shifts, mean_rows - shifts], axis=1).reshape(N_SEQ)
            loads = jnp.zeros((N_SEQ,), jnp.int32).at[owner_perm].set(paired)
            perm_keys = jax.random.split(jax.random.fold_in(block_key, 2), N_SEQ)
            cluster_perm = jax.vmap(lambda k: jax.random.permutation(k, local_clusters).astype(jnp.int32))(perm_keys)
            candidates = owner_order[:, None] * local_clusters + cluster_perm[:, slot_order // CAP]
            valid = slot_order[None, :] < loads[:, None]
            order_key = jnp.where(valid.reshape(-1), 0, 1).astype(jnp.int32) * (N_SEQ * owner_slots) + flat_order
            picked_index = jnp.argsort(order_key)[:TOK_DEV]
            picked = candidates.reshape(-1)[picked_index]
            token_perm = jax.random.permutation(jax.random.fold_in(block_key, 3), TOK_DEV)
            return picked[token_perm].astype(jnp.int32)
        block_keys = jax.vmap(lambda b: jax.random.fold_in(group_key, 100 + b))(jnp.arange(N_SEQ, dtype=jnp.int32))
        return jax.vmap(one_block)(block_keys).reshape(TOKENS)
    base_key = jax.random.fold_in(key, 7)
    groups = jax.vmap(lambda g: one_group(jax.random.fold_in(base_key, g)))(jnp.arange(GROUPS, dtype=jnp.int32))
    return groups[:, :, None].astype(jnp.int32)


def block_levels(key, extent, shards, smallest, top_value):
    level = 1.0
    for position, blocks in shards:
        draws = jax.random.uniform(jax.random.fold_in(jax.random.fold_in(key, 6), position), (blocks,), jnp.float32, smallest / len(shards), top_value / len(shards))
        level = level * jnp.repeat(jnp.exp(draws), extent[position] // blocks).reshape((-1,) + (1,) * (len(extent) - 1 - position))
    return level


def scatter_about(own_key, extent, deviation, reach, shards=(), kind=jnp.bfloat16):
    result = jax.random.normal(own_key, extent, jnp.float32) * deviation
    if len(shards) > 0:
        result = block_levels(own_key, extent, shards, -0.22, 0.18) * result
    return jnp.clip(result, min=-reach, max=reach).astype(kind)


def setup_inputs(seed: int = 0) -> dict:
    splits = jax.random.split(jax.random.key(seed), 6)
    queries = draw_queries(jax.random.fold_in(splits[5], 71), 0)
    keys = draw_keys(jax.random.fold_in(splits[5], 71), 0)
    values = scatter_about(splits[2], (TOKENS, HEADS * HD), 1.0, 6.0, ((0, 32), (1, 4)))
    cluster_ids = draw_cluster_ids(jax.random.fold_in(splits[5], 71), 0)
    w_out = scatter_about(splits[4], (HEADS * HD, D), (HEADS * HD) ** -0.5, 0.078125, ((0, 4),))
    return {"queries": queries, "keys": keys, "values": values, "cluster_ids": cluster_ids, "w_out": w_out}


def rank_slots(cluster):
    order = jnp.arange(cluster.shape[0], dtype=jnp.int32)
    same_cluster = cluster[:, None] == cluster[None, :]
    earlier = order[None, :] < order[:, None]
    ranking = lax.optimization_barrier(jnp.sum((same_cluster & earlier).astype(jnp.int32), axis=1))
    return (cluster * CAP + ranking).astype(jnp.int32)

def attend(queries, keys, values, counts):
    batch, rows_all, features = queries.shape
    heads_here = features // HD
    capacity = rows_all // counts.shape[1]
    head_shape = (batch, rows_all, heads_here, HD)
    scores = jnp.einsum('bqhd,bkhd->bhqk', queries.reshape(head_shape).astype(jnp.float32), keys.reshape(head_shape).astype(jnp.float32)) * (1.0 / math.sqrt(HD))
    key_order = jnp.arange(rows_all, dtype=jnp.int32)
    filled = jnp.repeat(counts.astype(jnp.float32), capacity, axis=1)
    present = (key_order % capacity).astype(jnp.float32)[None, :] < filled
    causal = key_order[None, :] <= key_order[:, None]
    diagonal_on = key_order[None, :] == key_order[:, None]
    allowed = present[:, None, None, :] & causal[None, None] | diagonal_on[None, None]
    scores = jnp.where(allowed, scores, -1e+30)
    row_max = lax.optimization_barrier(jnp.max(scores, axis=-1, keepdims=True))
    exp_scores = jnp.exp(scores - row_max)
    totals = lax.optimization_barrier(jnp.sum(exp_scores, axis=-1))
    weights = exp_scores.astype(jnp.bfloat16).astype(jnp.float32)
    attended = jnp.einsum('bhqk,bkhd->bqhd', weights, values.reshape(head_shape).astype(jnp.float32))
    attended = attended / jnp.transpose(totals, (0, 2, 1))[..., None]
    return attended.astype(jnp.bfloat16).reshape(batch, rows_all, features)

def reference(queries, keys, values, cluster_ids, w_out):
    heads_group = HEADS // N_HEAD
    features = heads_group * HD
    source_rows = jnp.arange(N_SEQ, dtype=jnp.int32)[:, None]
    accum = jnp.zeros((N_SEQ * TOK_DEV, D), jnp.float32)
    for group_index in range(N_HEAD):
        first_col = group_index * features
        cluster = cluster_ids[group_index, :, 0].reshape(N_SEQ, TOK_DEV)
        slot_index = jax.vmap(rank_slots)(cluster)
        tallies = lax.optimization_barrier(jnp.sum((cluster[:, :, None] == jnp.arange(NCLUST, dtype=jnp.int32)[None, None, :]).astype(jnp.int32), axis=1))

        def bucketize(block):
            part_block = block[:, first_col:first_col + features].reshape(N_SEQ, TOK_DEV, features)
            buffer = jnp.zeros((N_SEQ, NCLUST * CAP, features), jnp.bfloat16).at[source_rows, slot_index].set(part_block)
            return buffer.reshape(N_SEQ, NCLUST, CAP, features).transpose(1, 0, 2, 3).reshape(NCLUST, N_SEQ * CAP, features)

        def one_cluster(items):
            query_in, key_in, value_in, count_in = items
            return attend(query_in[None], key_in[None], value_in[None], count_in[None])[0]
        attended = lax.map(one_cluster, (bucketize(queries), bucketize(keys), bucketize(values), tallies.T))
        returned = attended.reshape(NCLUST, N_SEQ, CAP, features).transpose(1, 0, 2, 3).reshape(N_SEQ, NCLUST * CAP, features)
        own_rows = returned[source_rows, slot_index].reshape(N_SEQ * TOK_DEV, features)
        partial_value = jnp.dot(own_rows, w_out[first_col:first_col + features], preferred_element_type=jnp.float32)
        accum = accum + partial_value.astype(jnp.bfloat16).astype(jnp.float32)
    return accum.astype(jnp.bfloat16)
```

```python
import math

import jax
import jax.numpy as jnp
from jax import lax
from jax.sharding import PartitionSpec as P

HD = 128
NCLUST = 256
CAP = 4
OWNER_CAP = 24


def attend(queries, keys, values, counts):
    batch, rows_all, features = queries.shape
    heads_here = features // HD
    capacity = rows_all // counts.shape[1]
    head_shape = (batch, rows_all, heads_here, HD)
    scores = jnp.einsum(
        "bqhd,bkhd->bhqk",
        queries.reshape(head_shape),
        keys.reshape(head_shape),
        preferred_element_type=jnp.float32,
    ) * (1.0 / math.sqrt(HD))
    key_order = jnp.arange(rows_all, dtype=jnp.int32)
    filled = jnp.repeat(counts.astype(jnp.float32), capacity, axis=1)
    present = (key_order % capacity).astype(jnp.float32)[None, :] < filled
    causal = key_order[None, :] <= key_order[:, None]
    diagonal_on = key_order[None, :] == key_order[:, None]
    allowed = present[:, None, None, :] & causal[None, None] | diagonal_on[None, None]
    scores = jnp.where(allowed, scores, -1e30)
    row_max = jnp.max(scores, axis=-1, keepdims=True)
    exp_scores = jnp.exp(scores - row_max)
    totals = jnp.sum(exp_scores, axis=-1)
    weights = exp_scores.astype(jnp.bfloat16)
    attended = jnp.einsum(
        "bhqk,bkhd->bqhd", weights, values.reshape(head_shape), preferred_element_type=jnp.float32
    )
    attended = attended / jnp.transpose(totals, (0, 2, 1))[..., None]
    return attended.astype(jnp.bfloat16).reshape(batch, rows_all, features)


def body(queries, keys, values, cluster_ids, w_out):
    cluster = cluster_ids[0, :, 0]
    tokens = cluster.shape[0]
    seq_count = lax.axis_size("seq")
    cl_dev = NCLUST // seq_count
    features = queries.shape[1]
    rows = OWNER_CAP
    owner = cluster // cl_dev
    position = jnp.arange(tokens, dtype=jnp.int32)

    order_key = cluster * tokens + position
    same_owner = owner[:, None] == owner[None, :]
    before = order_key[None, :] < order_key[:, None]
    rank = jnp.sum((same_owner & before).astype(jnp.int32), axis=1)
    dest = owner * rows + rank

    slot = jnp.arange(seq_count * rows, dtype=jnp.int32)
    hit = dest[None, :] == slot[:, None]
    source_token = jnp.sum(jnp.where(hit, position[None, :], 0), axis=1)

    packed = jnp.concatenate([queries, keys, values], axis=1)
    outgoing = packed[source_token].reshape(seq_count, rows, 3 * features)
    counts = jnp.sum(
        (cluster[:, None] == jnp.arange(NCLUST, dtype=jnp.int32)[None, :]).astype(jnp.int32),
        axis=0,
    ).reshape(seq_count, cl_dev)

    incoming = lax.all_to_all(outgoing, "seq", 0, 0, tiled=True)
    count_in = lax.all_to_all(counts, "seq", 0, 0, tiled=True)

    ends = jnp.cumsum(count_in, axis=1)
    offset = ends - count_in
    r = jnp.arange(CAP, dtype=jnp.int32)
    src = jnp.arange(seq_count, dtype=jnp.int32)
    take = offset.T[:, :, None] + jnp.minimum(r[None, None, :], jnp.maximum(count_in.T[:, :, None] - 1, 0))
    take = jnp.clip(take, 0, rows - 1) + src[None, :, None] * rows
    flat_in = incoming.reshape(seq_count * rows, 3 * features)
    bucket = flat_in[take.reshape(-1)].reshape(cl_dev, seq_count * CAP, 3 * features)
    result = attend(
        bucket[:, :, :features],
        bucket[:, :, features : 2 * features],
        bucket[:, :, 2 * features :],
        count_in.T,
    )

    j = jnp.arange(rows, dtype=jnp.int32)
    c_of = jnp.sum((ends[:, None, :] <= j[None, :, None]).astype(jnp.int32), axis=2)
    c_of = jnp.minimum(c_of, cl_dev - 1)
    r_of = j[None, :] - jnp.take_along_axis(offset, c_of, axis=1)
    r_of = jnp.clip(r_of, 0, CAP - 1)
    back_index = c_of * (seq_count * CAP) + src[:, None] * CAP + r_of
    flat_result = result.reshape(cl_dev * seq_count * CAP, features)
    back = flat_result[back_index.reshape(-1)].reshape(seq_count, rows, features)
    returned = lax.all_to_all(back, "seq", 0, 0, tiled=True)

    own_rows = returned.reshape(seq_count * rows, features)[dest]
    partial_value = jnp.dot(own_rows, w_out, preferred_element_type=jnp.float32)
    summed = lax.psum_scatter(
        partial_value.astype(jnp.bfloat16), "head", scatter_dimension=1, tiled=True
    )
    return summed


def solution(mesh):
    return jax.shard_map(
        body,
        mesh=mesh,
        in_specs=(
            P("seq", "head"),
            P("seq", "head"),
            P("seq", "head"),
            P("head", "seq", None),
            P("head", None),
        ),
        out_specs=P("seq", "head"),
        check_vma=False,
    )
```

```python
import math

import jax
import jax.numpy as jnp
from jax import lax
from jax.sharding import PartitionSpec as P

HD = 128
NCLUST = 256
CAP = 4
OWNER_CAP = 24
NSPLIT = 2


def attend(queries, keys, values, counts):
    batch, rows_all, features = queries.shape
    heads_here = features // HD
    capacity = rows_all // counts.shape[1]
    head_shape = (batch, rows_all, heads_here, HD)
    scores = jnp.einsum(
        "bqhd,bkhd->bhqk",
        queries.reshape(head_shape),
        keys.reshape(head_shape),
        preferred_element_type=jnp.float32,
    ) * (1.0 / math.sqrt(HD))
    key_order = jnp.arange(rows_all, dtype=jnp.int32)
    filled = jnp.repeat(counts.astype(jnp.float32), capacity, axis=1)
    present = (key_order % capacity).astype(jnp.float32)[None, :] < filled
    causal = key_order[None, :] <= key_order[:, None]
    diagonal_on = key_order[None, :] == key_order[:, None]
    allowed = present[:, None, None, :] & causal[None, None] | diagonal_on[None, None]
    scores = jnp.where(allowed, scores, -1e30)
    row_max = jnp.max(scores, axis=-1, keepdims=True)
    exp_scores = jnp.exp(scores - row_max)
    totals = jnp.sum(exp_scores, axis=-1)
    weights = exp_scores.astype(jnp.bfloat16)
    attended = jnp.einsum(
        "bhqk,bkhd->bqhd", weights, values.reshape(head_shape), preferred_element_type=jnp.float32
    )
    attended = attended / jnp.transpose(totals, (0, 2, 1))[..., None]
    return attended.astype(jnp.bfloat16).reshape(batch, rows_all, features)


def one_hot(index, size):
    return (index[:, None] == jnp.arange(size, dtype=jnp.int32)[None, :]).astype(jnp.bfloat16)


def permute(selector, block):
    return jnp.dot(selector, block, preferred_element_type=jnp.float32).astype(jnp.bfloat16)


def body(queries, keys, values, cluster_ids, w_out):
    cluster = cluster_ids[0, :, 0]
    tokens = cluster.shape[0]
    seq_count = lax.axis_size("seq")
    cl_dev = NCLUST // seq_count
    features = queries.shape[1]
    heads_here = features // HD
    split = NSPLIT if heads_here % NSPLIT == 0 else 1
    part = features // split
    rows = OWNER_CAP
    slots = seq_count * rows
    bucket_rows = cl_dev * seq_count * CAP
    owner = cluster // cl_dev
    position = jnp.arange(tokens, dtype=jnp.int32)

    order_key = cluster * tokens + position
    same_owner = owner[:, None] == owner[None, :]
    before = order_key[None, :] < order_key[:, None]
    rank = jnp.sum((same_owner & before).astype(jnp.int32), axis=1)
    dest = owner * rows + rank
    to_token = one_hot(dest, slots)
    to_slot = to_token.T

    all_clusters = lax.all_gather(cluster, "seq", tiled=True).reshape(seq_count, tokens)
    me = lax.axis_index("seq")
    local = jnp.arange(cl_dev, dtype=jnp.int32) + me * cl_dev
    count_in = jnp.sum(
        (all_clusters[:, :, None] == local[None, None, :]).astype(jnp.int32), axis=1
    )

    ends = jnp.cumsum(count_in, axis=1)
    offset = ends - count_in
    r = jnp.arange(CAP, dtype=jnp.int32)
    src = jnp.arange(seq_count, dtype=jnp.int32)
    take = offset.T[:, :, None] + jnp.minimum(r[None, None, :], jnp.maximum(count_in.T[:, :, None] - 1, 0))
    take = jnp.clip(take, 0, rows - 1) + src[None, :, None] * rows
    to_bucket = one_hot(take.reshape(-1), slots)

    j = jnp.arange(rows, dtype=jnp.int32)
    c_of = jnp.sum((ends[:, None, :] <= j[None, :, None]).astype(jnp.int32), axis=2)
    c_of = jnp.minimum(c_of, cl_dev - 1)
    r_of = j[None, :] - jnp.take_along_axis(offset, c_of, axis=1)
    r_of = jnp.clip(r_of, 0, CAP - 1)
    back_index = c_of * (seq_count * CAP) + src[:, None] * CAP + r_of
    to_compact = one_hot(back_index.reshape(-1), bucket_rows)

    partial_value = None
    for k in range(split):
        cols = slice(k * part, (k + 1) * part)
        packed = jnp.concatenate([queries[:, cols], keys[:, cols], values[:, cols]], axis=1)
        outgoing = permute(to_slot, packed).reshape(seq_count, rows, 3 * part)
        incoming = lax.all_to_all(outgoing, "seq", 0, 0, tiled=True).reshape(slots, 3 * part)
        shape = (cl_dev, seq_count * CAP, part)
        result = attend(
            permute(to_bucket, incoming[:, :part]).reshape(shape),
            permute(to_bucket, incoming[:, part : 2 * part]).reshape(shape),
            permute(to_bucket, incoming[:, 2 * part :]).reshape(shape),
            count_in.T,
        )
        back = permute(to_compact, result.reshape(bucket_rows, part))
        returned = lax.all_to_all(back.reshape(seq_count, rows, part), "seq", 0, 0, tiled=True)
        own_rows = permute(to_token, returned.reshape(slots, part))
        term = jnp.dot(own_rows, w_out[cols], preferred_element_type=jnp.float32)
        partial_value = term if partial_value is None else partial_value + term
    summed = lax.psum_scatter(
        partial_value.astype(jnp.bfloat16), "head", scatter_dimension=1, tiled=True
    )
    return summed


def solution(mesh):
    return jax.shard_map(
        body,
        mesh=mesh,
        in_specs=(
            P("seq", "head"),
            P("seq", "head"),
            P("seq", "head"),
            P("head", "seq", None),
            P("head", None),
        ),
        out_specs=P("seq", "head"),
        check_vma=False,
    )
```

```python
import math

import jax
import jax.numpy as jnp
from jax import lax
from jax.sharding import PartitionSpec as P

HD = 128
NCLUST = 256
CAP = 4
OWNER_CAP = 24
NSPLIT = 2


def attend(queries, keys, values, counts):
    batch, rows_all, features = queries.shape
    heads_here = features // HD
    capacity = rows_all // counts.shape[1]
    head_shape = (batch, rows_all, heads_here, HD)
    scores = jnp.einsum(
        "bqhd,bkhd->bhqk",
        queries.reshape(head_shape),
        keys.reshape(head_shape),
        preferred_element_type=jnp.float32,
    ) * (1.0 / math.sqrt(HD))
    key_order = jnp.arange(rows_all, dtype=jnp.int32)
    filled = jnp.repeat(counts.astype(jnp.float32), capacity, axis=1)
    present = (key_order % capacity).astype(jnp.float32)[None, :] < filled
    causal = key_order[None, :] <= key_order[:, None]
    diagonal_on = key_order[None, :] == key_order[:, None]
    allowed = present[:, None, None, :] & causal[None, None] | diagonal_on[None, None]
    scores = jnp.where(allowed, scores, -1e30)
    row_max = jnp.max(scores, axis=-1, keepdims=True)
    exp_scores = jnp.exp(scores - row_max)
    totals = jnp.sum(exp_scores, axis=-1)
    weights = exp_scores.astype(jnp.bfloat16)
    attended = jnp.einsum(
        "bhqk,bkhd->bqhd", weights, values.reshape(head_shape), preferred_element_type=jnp.float32
    )
    attended = attended / jnp.transpose(totals, (0, 2, 1))[..., None]
    return attended.astype(jnp.bfloat16).reshape(batch, rows_all, features)


def attend_heads(queries, keys, values, counts):
    heads_here, batch, rows_all, _ = queries.shape
    capacity = rows_all // counts.shape[1]
    scores = jnp.einsum(
        "hbqd,hbkd->hbqk", queries, keys, preferred_element_type=jnp.float32
    ) * (1.0 / math.sqrt(HD))
    key_order = jnp.arange(rows_all, dtype=jnp.int32)
    filled = jnp.repeat(counts.astype(jnp.float32), capacity, axis=1)
    present = (key_order % capacity).astype(jnp.float32)[None, :] < filled
    causal = key_order[None, :] <= key_order[:, None]
    diagonal_on = key_order[None, :] == key_order[:, None]
    allowed = present[:, None, :] & causal[None] | diagonal_on[None]
    scores = jnp.where(allowed[None], scores, -1e30)
    row_max = jnp.max(scores, axis=-1, keepdims=True)
    exp_scores = jnp.exp(scores - row_max)
    totals = jnp.sum(exp_scores, axis=-1, keepdims=True)
    weights = exp_scores.astype(jnp.bfloat16)
    attended = jnp.einsum("hbqk,hbkd->hbqd", weights, values, preferred_element_type=jnp.float32)
    attended = attended / totals
    return attended.astype(jnp.bfloat16).reshape(heads_here, batch * rows_all, HD)


def one_hot(index, size):
    return (index[:, None] == jnp.arange(size, dtype=jnp.int32)[None, :]).astype(jnp.bfloat16)


def permute(selector, block):
    return jnp.dot(selector, block, preferred_element_type=jnp.float32).astype(jnp.bfloat16)


def body(queries, keys, values, cluster_ids, w_out):
    cluster = cluster_ids[0, :, 0]
    tokens = cluster.shape[0]
    seq_count = lax.axis_size("seq")
    cl_dev = NCLUST // seq_count
    features = queries.shape[1]
    heads_here = features // HD
    split = NSPLIT if heads_here % NSPLIT == 0 else 1
    part = features // split
    rows = OWNER_CAP
    slots = seq_count * rows
    bucket_rows = cl_dev * seq_count * CAP
    owner = cluster // cl_dev
    position = jnp.arange(tokens, dtype=jnp.int32)

    order_key = cluster * tokens + position
    same_owner = owner[:, None] == owner[None, :]
    before = order_key[None, :] < order_key[:, None]
    rank = jnp.sum((same_owner & before).astype(jnp.int32), axis=1)
    dest = owner * rows + rank
    to_token = one_hot(dest, slots)
    to_slot = to_token.T

    counts = jnp.sum(
        (cluster[:, None] == jnp.arange(NCLUST, dtype=jnp.int32)[None, :]).astype(jnp.int32),
        axis=0,
    ).reshape(seq_count, cl_dev)
    count_in = lax.all_to_all(counts, "seq", 0, 0, tiled=True)

    ends = jnp.cumsum(count_in, axis=1)
    offset = ends - count_in
    r = jnp.arange(CAP, dtype=jnp.int32)
    src = jnp.arange(seq_count, dtype=jnp.int32)
    take = offset.T[:, :, None] + jnp.minimum(r[None, None, :], jnp.maximum(count_in.T[:, :, None] - 1, 0))
    take = jnp.clip(take, 0, rows - 1) + src[None, :, None] * rows
    to_bucket = one_hot(take.reshape(-1), slots)

    j = jnp.arange(rows, dtype=jnp.int32)
    c_of = jnp.sum((ends[:, None, :] <= j[None, :, None]).astype(jnp.int32), axis=2)
    c_of = jnp.minimum(c_of, cl_dev - 1)
    r_of = j[None, :] - jnp.take_along_axis(offset, c_of, axis=1)
    r_of = jnp.clip(r_of, 0, CAP - 1)
    back_index = c_of * (seq_count * CAP) + src[:, None] * CAP + r_of
    to_compact = one_hot(back_index.reshape(-1), bucket_rows)

    partial_value = None
    for k in range(split):
        cols = slice(k * part, (k + 1) * part)
        packed = jnp.concatenate([queries[:, cols], keys[:, cols], values[:, cols]], axis=1)
        outgoing = permute(to_slot, packed).reshape(seq_count, rows, 3 * part)
        incoming = lax.all_to_all(outgoing, "seq", 0, 0, tiled=True).reshape(slots, 3 * part)
        heads_part = part // HD
        def bucketize(block):
            picked = jnp.einsum(
                "rs,shd->hrd",
                to_bucket,
                block.reshape(slots, heads_part, HD),
                preferred_element_type=jnp.float32,
            ).astype(jnp.bfloat16)
            return picked.reshape(heads_part, cl_dev, seq_count * CAP, HD)

        result = attend_heads(
            bucketize(incoming[:, :part]),
            bucketize(incoming[:, part : 2 * part]),
            bucketize(incoming[:, 2 * part :]),
            count_in.T,
        )
        back = jnp.einsum(
            "rb,hbd->rhd", to_compact, result, preferred_element_type=jnp.float32
        ).astype(jnp.bfloat16).reshape(slots, part)
        returned = lax.all_to_all(back.reshape(seq_count, rows, part), "seq", 0, 0, tiled=True)
        own_rows = permute(to_token, returned.reshape(slots, part))
        term = jnp.dot(own_rows, w_out[cols], preferred_element_type=jnp.float32)
        partial_value = term if partial_value is None else partial_value + term
    summed = lax.psum_scatter(
        partial_value.astype(jnp.bfloat16), "head", scatter_dimension=1, tiled=True
    )
    return summed


def solution(mesh):
    return jax.shard_map(
        body,
        mesh=mesh,
        in_specs=(
            P("seq", "head"),
            P("seq", "head"),
            P("seq", "head"),
            P("head", "seq", None),
            P("head", None),
        ),
        out_specs=P("seq", "head"),
        check_vma=False,
    )
```

```python
import math

import jax
import jax.numpy as jnp
from jax import lax
from jax.sharding import PartitionSpec as P

HD = 128
NCLUST = 256
CAP = 4
OWNER_CAP = 24
NSPLIT = 2


def attend(queries, keys, values, counts):
    batch, rows_all, features = queries.shape
    heads_here = features // HD
    capacity = rows_all // counts.shape[1]
    head_shape = (batch, rows_all, heads_here, HD)
    scores = jnp.einsum(
        "bqhd,bkhd->bhqk",
        queries.reshape(head_shape),
        keys.reshape(head_shape),
        preferred_element_type=jnp.float32,
    ) * (1.0 / math.sqrt(HD))
    key_order = jnp.arange(rows_all, dtype=jnp.int32)
    filled = jnp.repeat(counts.astype(jnp.float32), capacity, axis=1)
    present = (key_order % capacity).astype(jnp.float32)[None, :] < filled
    causal = key_order[None, :] <= key_order[:, None]
    diagonal_on = key_order[None, :] == key_order[:, None]
    allowed = present[:, None, None, :] & causal[None, None] | diagonal_on[None, None]
    scores = jnp.where(allowed, scores, -1e30)
    row_max = jnp.max(scores, axis=-1, keepdims=True)
    exp_scores = jnp.exp(scores - row_max)
    totals = jnp.sum(exp_scores, axis=-1)
    weights = exp_scores.astype(jnp.bfloat16)
    attended = jnp.einsum(
        "bhqk,bkhd->bqhd", weights, values.reshape(head_shape), preferred_element_type=jnp.float32
    )
    attended = attended / jnp.transpose(totals, (0, 2, 1))[..., None]
    return attended.astype(jnp.bfloat16).reshape(batch, rows_all, features)


def attend_heads(queries, keys, values, counts):
    heads_here, batch, rows_all, _ = queries.shape
    capacity = rows_all // counts.shape[1]
    scores = jnp.einsum(
        "hbqd,hbkd->hbqk", queries, keys, preferred_element_type=jnp.float32
    ) * (1.0 / math.sqrt(HD))
    key_order = jnp.arange(rows_all, dtype=jnp.int32)
    filled = jnp.repeat(counts.astype(jnp.float32), capacity, axis=1)
    present = (key_order % capacity).astype(jnp.float32)[None, :] < filled
    causal = key_order[None, :] <= key_order[:, None]
    diagonal_on = key_order[None, :] == key_order[:, None]
    allowed = present[:, None, :] & causal[None] | diagonal_on[None]
    scores = jnp.where(allowed[None], scores, -1e30)
    row_max = jnp.max(scores, axis=-1, keepdims=True)
    exp_scores = jnp.exp(scores - row_max)
    totals = jnp.sum(exp_scores, axis=-1, keepdims=True)
    weights = exp_scores.astype(jnp.bfloat16)
    attended = jnp.einsum("hbqk,hbkd->hbqd", weights, values, preferred_element_type=jnp.float32)
    attended = attended / totals
    return attended.astype(jnp.bfloat16).reshape(heads_here, batch * rows_all, HD)


def one_hot(index, size):
    return (index[:, None] == jnp.arange(size, dtype=jnp.int32)[None, :]).astype(jnp.bfloat16)


def permute(selector, block):
    return jnp.dot(selector, block, preferred_element_type=jnp.float32).astype(jnp.bfloat16)


def body(queries, keys, values, cluster_ids, w_out):
    cluster = cluster_ids[0, :, 0]
    tokens = cluster.shape[0]
    seq_count = lax.axis_size("seq")
    cl_dev = NCLUST // seq_count
    features = queries.shape[1]
    heads_here = features // HD
    split = NSPLIT if heads_here % NSPLIT == 0 else 1
    part = features // split
    rows = OWNER_CAP
    slots = seq_count * rows
    bucket_rows = cl_dev * seq_count * CAP
    owner = cluster // cl_dev
    position = jnp.arange(tokens, dtype=jnp.int32)

    order_key = cluster * tokens + position
    same_owner = owner[:, None] == owner[None, :]
    before = order_key[None, :] < order_key[:, None]
    rank = jnp.sum((same_owner & before).astype(jnp.int32), axis=1)
    dest = owner * rows + rank
    to_token = one_hot(dest, slots)
    to_slot = to_token.T

    counts = jnp.sum(
        (cluster[:, None] == jnp.arange(NCLUST, dtype=jnp.int32)[None, :]).astype(jnp.int32),
        axis=0,
    ).reshape(seq_count, cl_dev)
    count_in = lax.all_to_all(counts, "seq", 0, 0, tiled=True)

    ends = jnp.cumsum(count_in, axis=1)
    offset = ends - count_in
    r = jnp.arange(CAP, dtype=jnp.int32)
    src = jnp.arange(seq_count, dtype=jnp.int32)
    take = offset.T[:, :, None] + jnp.minimum(r[None, None, :], jnp.maximum(count_in.T[:, :, None] - 1, 0))
    take = jnp.clip(take, 0, rows - 1) + src[None, :, None] * rows
    to_bucket = one_hot(take.reshape(-1), slots)

    j = jnp.arange(rows, dtype=jnp.int32)
    c_of = jnp.sum((ends[:, None, :] <= j[None, :, None]).astype(jnp.int32), axis=2)
    c_of = jnp.minimum(c_of, cl_dev - 1)
    r_of = j[None, :] - jnp.take_along_axis(offset, c_of, axis=1)
    r_of = jnp.clip(r_of, 0, CAP - 1)
    back_index = c_of * (seq_count * CAP) + src[:, None] * CAP + r_of
    to_compact = one_hot(back_index.reshape(-1), bucket_rows)

    outgoing_all = []
    for k in range(split):
        cols = slice(k * part, (k + 1) * part)
        packed = jnp.concatenate([queries[:, cols], keys[:, cols], values[:, cols]], axis=1)
        outgoing_all.append(permute(to_slot, packed).reshape(seq_count, rows, 3 * part))

    partial_value = None
    for k in range(split):
        cols = slice(k * part, (k + 1) * part)
        outgoing = outgoing_all[k]
        if k == 1:
            outgoing, to_bucket, to_compact = lax.optimization_barrier(
                (outgoing, to_bucket, to_compact)
            )
        incoming = lax.all_to_all(outgoing, "seq", 0, 0, tiled=True).reshape(slots, 3 * part)
        heads_part = part // HD
        def bucketize(block):
            picked = jnp.einsum(
                "rs,shd->hrd",
                to_bucket,
                block.reshape(slots, heads_part, HD),
                preferred_element_type=jnp.float32,
            ).astype(jnp.bfloat16)
            return picked.reshape(heads_part, cl_dev, seq_count * CAP, HD)

        result = attend_heads(
            bucketize(incoming[:, :part]),
            bucketize(incoming[:, part : 2 * part]),
            bucketize(incoming[:, 2 * part :]),
            count_in.T,
        )
        back = jnp.einsum(
            "rb,hbd->rhd", to_compact, result, preferred_element_type=jnp.float32
        ).astype(jnp.bfloat16).reshape(slots, part)
        returned = lax.all_to_all(back.reshape(seq_count, rows, part), "seq", 0, 0, tiled=True)
        own_rows = permute(to_token, returned.reshape(slots, part))
        term = jnp.dot(own_rows, w_out[cols], preferred_element_type=jnp.float32)
        partial_value = term if partial_value is None else partial_value + term
    summed = lax.psum_scatter(
        partial_value.astype(jnp.bfloat16), "head", scatter_dimension=1, tiled=True
    )
    return summed


def solution(mesh):
    return jax.shard_map(
        body,
        mesh=mesh,
        in_specs=(
            P("seq", "head"),
            P("seq", "head"),
            P("seq", "head"),
            P("head", "seq", None),
            P("head", None),
        ),
        out_specs=P("seq", "head"),
        check_vma=False,
    )
```

```python
import math

import jax
import jax.numpy as jnp
from jax import lax
from jax.sharding import PartitionSpec as P

HD = 128
NCLUST = 256
CAP = 4
OWNER_CAP = 24
NSPLIT = 3


def attend(queries, keys, values, counts):
    batch, rows_all, features = queries.shape
    heads_here = features // HD
    capacity = rows_all // counts.shape[1]
    head_shape = (batch, rows_all, heads_here, HD)
    scores = jnp.einsum(
        "bqhd,bkhd->bhqk",
        queries.reshape(head_shape),
        keys.reshape(head_shape),
        preferred_element_type=jnp.float32,
    ) * (1.0 / math.sqrt(HD))
    key_order = jnp.arange(rows_all, dtype=jnp.int32)
    filled = jnp.repeat(counts.astype(jnp.float32), capacity, axis=1)
    present = (key_order % capacity).astype(jnp.float32)[None, :] < filled
    causal = key_order[None, :] <= key_order[:, None]
    diagonal_on = key_order[None, :] == key_order[:, None]
    allowed = present[:, None, None, :] & causal[None, None] | diagonal_on[None, None]
    scores = jnp.where(allowed, scores, -1e30)
    row_max = jnp.max(scores, axis=-1, keepdims=True)
    exp_scores = jnp.exp(scores - row_max)
    totals = jnp.sum(exp_scores, axis=-1)
    weights = exp_scores.astype(jnp.bfloat16)
    attended = jnp.einsum(
        "bhqk,bkhd->bqhd", weights, values.reshape(head_shape), preferred_element_type=jnp.float32
    )
    attended = attended / jnp.transpose(totals, (0, 2, 1))[..., None]
    return attended.astype(jnp.bfloat16).reshape(batch, rows_all, features)


def attend_heads(queries, keys, values, counts):
    heads_here, batch, rows_all, _ = queries.shape
    capacity = rows_all // counts.shape[1]
    scores = jnp.einsum(
        "hbqd,hbkd->hbqk", queries, keys, preferred_element_type=jnp.float32
    ) * (1.0 / math.sqrt(HD))
    key_order = jnp.arange(rows_all, dtype=jnp.int32)
    filled = jnp.repeat(counts.astype(jnp.float32), capacity, axis=1)
    present = (key_order % capacity).astype(jnp.float32)[None, :] < filled
    causal = key_order[None, :] <= key_order[:, None]
    diagonal_on = key_order[None, :] == key_order[:, None]
    allowed = present[:, None, :] & causal[None] | diagonal_on[None]
    scores = jnp.where(allowed[None], scores, -1e30)
    row_max = jnp.max(scores, axis=-1, keepdims=True)
    exp_scores = jnp.exp(scores - row_max)
    totals = jnp.sum(exp_scores, axis=-1, keepdims=True)
    weights = exp_scores.astype(jnp.bfloat16)
    attended = jnp.einsum("hbqk,hbkd->hbqd", weights, values, preferred_element_type=jnp.float32)
    attended = attended / totals
    return attended.astype(jnp.bfloat16).reshape(heads_here, batch * rows_all, HD)


def one_hot(index, size):
    return (index[:, None] == jnp.arange(size, dtype=jnp.int32)[None, :]).astype(jnp.bfloat16)


def permute(selector, block):
    return jnp.dot(selector, block, preferred_element_type=jnp.float32).astype(jnp.bfloat16)


def body(queries, keys, values, cluster_ids, w_out):
    cluster = cluster_ids[0, :, 0]
    tokens = cluster.shape[0]
    seq_count = lax.axis_size("seq")
    cl_dev = NCLUST // seq_count
    features = queries.shape[1]
    heads_here = features // HD
    split = NSPLIT if heads_here % NSPLIT == 0 else 1
    part = features // split
    rows = OWNER_CAP
    slots = seq_count * rows
    bucket_rows = cl_dev * seq_count * CAP
    owner = cluster // cl_dev
    position = jnp.arange(tokens, dtype=jnp.int32)

    order_key = cluster * tokens + position
    same_owner = owner[:, None] == owner[None, :]
    before = order_key[None, :] < order_key[:, None]
    rank = jnp.sum((same_owner & before).astype(jnp.int32), axis=1)
    dest = owner * rows + rank
    to_token = one_hot(dest, slots)
    to_slot = to_token.T

    counts = jnp.sum(
        (cluster[:, None] == jnp.arange(NCLUST, dtype=jnp.int32)[None, :]).astype(jnp.int32),
        axis=0,
    ).reshape(seq_count, cl_dev)
    count_in = lax.all_to_all(counts, "seq", 0, 0, tiled=True)

    ends = jnp.cumsum(count_in, axis=1)
    offset = ends - count_in
    r = jnp.arange(CAP, dtype=jnp.int32)
    src = jnp.arange(seq_count, dtype=jnp.int32)
    take = offset.T[:, :, None] + jnp.minimum(r[None, None, :], jnp.maximum(count_in.T[:, :, None] - 1, 0))
    take = jnp.clip(take, 0, rows - 1) + src[None, :, None] * rows
    to_bucket = one_hot(take.reshape(-1), slots)

    j = jnp.arange(rows, dtype=jnp.int32)
    c_of = jnp.sum((ends[:, None, :] <= j[None, :, None]).astype(jnp.int32), axis=2)
    c_of = jnp.minimum(c_of, cl_dev - 1)
    r_of = j[None, :] - jnp.take_along_axis(offset, c_of, axis=1)
    r_of = jnp.clip(r_of, 0, CAP - 1)
    back_index = c_of * (seq_count * CAP) + src[:, None] * CAP + r_of
    to_compact = one_hot(back_index.reshape(-1), bucket_rows)

    outgoing_all = []
    for k in range(split):
        cols = slice(k * part, (k + 1) * part)
        packed = jnp.concatenate([queries[:, cols], keys[:, cols], values[:, cols]], axis=1)
        outgoing_all.append(permute(to_slot, packed).reshape(seq_count, rows, 3 * part))

    partial_value = None
    for k in range(split):
        cols = slice(k * part, (k + 1) * part)
        outgoing = outgoing_all[k]
        if k == 1:
            outgoing, to_bucket, to_compact = lax.optimization_barrier(
                (outgoing, to_bucket, to_compact)
            )
        incoming = lax.all_to_all(outgoing, "seq", 0, 0, tiled=True).reshape(slots, 3 * part)
        heads_part = part // HD
        def bucketize(block):
            picked = jnp.einsum(
                "rs,shd->hrd",
                to_bucket,
                block.reshape(slots, heads_part, HD),
                preferred_element_type=jnp.float32,
            ).astype(jnp.bfloat16)
            return picked.reshape(heads_part, cl_dev, seq_count * CAP, HD)

        result = attend_heads(
            bucketize(incoming[:, :part]),
            bucketize(incoming[:, part : 2 * part]),
            bucketize(incoming[:, 2 * part :]),
            count_in.T,
        )
        back = jnp.einsum(
            "rb,hbd->rhd", to_compact, result, preferred_element_type=jnp.float32
        ).astype(jnp.bfloat16).reshape(slots, part)
        returned = lax.all_to_all(back.reshape(seq_count, rows, part), "seq", 0, 0, tiled=True)
        own_rows = permute(to_token, returned.reshape(slots, part))
        term = jnp.dot(own_rows, w_out[cols], preferred_element_type=jnp.float32)
        partial_value = term if partial_value is None else partial_value + term
    summed = lax.psum_scatter(
        partial_value.astype(jnp.bfloat16), "head", scatter_dimension=1, tiled=True
    )
    return summed


def solution(mesh):
    return jax.shard_map(
        body,
        mesh=mesh,
        in_specs=(
            P("seq", "head"),
            P("seq", "head"),
            P("seq", "head"),
            P("head", "seq", None),
            P("head", None),
        ),
        out_specs=P("seq", "head"),
        check_vma=False,
    )
```

```python
import math

import jax
import jax.numpy as jnp
from jax import lax
from jax.sharding import PartitionSpec as P

HD = 128
NCLUST = 256
CAP = 4
OWNER_CAP = 24
NSPLIT = 2


def attend(queries, keys, values, counts):
    batch, rows_all, features = queries.shape
    heads_here = features // HD
    capacity = rows_all // counts.shape[1]
    head_shape = (batch, rows_all, heads_here, HD)
    scores = jnp.einsum(
        "bqhd,bkhd->bhqk",
        queries.reshape(head_shape),
        keys.reshape(head_shape),
        preferred_element_type=jnp.float32,
    ) * (1.0 / math.sqrt(HD))
    key_order = jnp.arange(rows_all, dtype=jnp.int32)
    filled = jnp.repeat(counts.astype(jnp.float32), capacity, axis=1)
    present = (key_order % capacity).astype(jnp.float32)[None, :] < filled
    causal = key_order[None, :] <= key_order[:, None]
    diagonal_on = key_order[None, :] == key_order[:, None]
    allowed = present[:, None, None, :] & causal[None, None] | diagonal_on[None, None]
    scores = jnp.where(allowed, scores, -1e30)
    row_max = jnp.max(scores, axis=-1, keepdims=True)
    exp_scores = jnp.exp(scores - row_max)
    totals = jnp.sum(exp_scores, axis=-1)
    weights = exp_scores.astype(jnp.bfloat16)
    attended = jnp.einsum(
        "bhqk,bkhd->bqhd", weights, values.reshape(head_shape), preferred_element_type=jnp.float32
    )
    attended = attended / jnp.transpose(totals, (0, 2, 1))[..., None]
    return attended.astype(jnp.bfloat16).reshape(batch, rows_all, features)


def attend_heads(queries, keys, values, counts):
    heads_here, batch, rows_all, _ = queries.shape
    capacity = rows_all // counts.shape[1]
    scores = jnp.einsum(
        "hbqd,hbkd->hbqk", queries, keys, preferred_element_type=jnp.float32
    ) * (1.0 / math.sqrt(HD))
    key_order = jnp.arange(rows_all, dtype=jnp.int32)
    filled = jnp.repeat(counts.astype(jnp.float32), capacity, axis=1)
    present = (key_order % capacity).astype(jnp.float32)[None, :] < filled
    causal = key_order[None, :] <= key_order[:, None]
    diagonal_on = key_order[None, :] == key_order[:, None]
    allowed = present[:, None, :] & causal[None] | diagonal_on[None]
    scores = jnp.where(allowed[None], scores, -1e30)
    row_max = jnp.max(scores, axis=-1, keepdims=True)
    exp_scores = jnp.exp(scores - row_max)
    totals = jnp.sum(exp_scores, axis=-1, keepdims=True)
    weights = exp_scores.astype(jnp.bfloat16)
    attended = jnp.einsum("hbqk,hbkd->hbqd", weights, values, preferred_element_type=jnp.float32)
    attended = attended / totals
    return attended.astype(jnp.bfloat16).reshape(heads_here, batch * rows_all, HD)


def one_hot(index, size):
    return (index[:, None] == jnp.arange(size, dtype=jnp.int32)[None, :]).astype(jnp.bfloat16)


def permute(selector, block):
    return jnp.dot(selector, block, preferred_element_type=jnp.float32).astype(jnp.bfloat16)


def body(queries, keys, values, cluster_ids, w_out):
    cluster = cluster_ids[0, :, 0]
    tokens = cluster.shape[0]
    seq_count = lax.axis_size("seq")
    cl_dev = NCLUST // seq_count
    features = queries.shape[1]
    heads_here = features // HD
    split = NSPLIT if heads_here % NSPLIT == 0 else 1
    part = features // split
    rows = OWNER_CAP
    slots = seq_count * rows
    bucket_rows = cl_dev * seq_count * CAP
    owner = cluster // cl_dev
    position = jnp.arange(tokens, dtype=jnp.int32)

    order_key = cluster * tokens + position
    same_owner = owner[:, None] == owner[None, :]
    before = order_key[None, :] < order_key[:, None]
    rank = jnp.sum((same_owner & before).astype(jnp.int32), axis=1)
    dest = owner * rows + rank
    to_token = one_hot(dest, slots)
    to_slot = to_token.T

    counts = jnp.sum(
        (cluster[:, None] == jnp.arange(NCLUST, dtype=jnp.int32)[None, :]).astype(jnp.int32),
        axis=0,
    ).reshape(seq_count, cl_dev)
    count_in = lax.all_to_all(counts, "seq", 0, 0, tiled=True)

    ends = jnp.cumsum(count_in, axis=1)
    j = jnp.arange(rows, dtype=jnp.int32)
    c_of = jnp.sum((ends[:, None, :] <= j[None, :, None]).astype(jnp.int32), axis=2)
    row_cluster = c_of.reshape(slots)
    valid = row_cluster < cl_dev
    flat = jnp.arange(slots, dtype=jnp.int32)
    allowed = (
        (row_cluster[:, None] == row_cluster[None, :])
        & valid[None, :]
        & (flat[None, :] <= flat[:, None])
    ) | (flat[None, :] == flat[:, None])

    partial_value = None
    for k in range(split):
        cols = slice(k * part, (k + 1) * part)
        packed = jnp.concatenate([queries[:, cols], keys[:, cols], values[:, cols]], axis=1)
        outgoing = permute(to_slot, packed).reshape(seq_count, rows, 3 * part)
        incoming = lax.all_to_all(outgoing, "seq", 0, 0, tiled=True).reshape(slots, 3 * part)
        heads_part = part // HD
        head_shape = (slots, heads_part, HD)
        scores = jnp.einsum(
            "qhd,khd->hqk",
            incoming[:, :part].reshape(head_shape),
            incoming[:, part : 2 * part].reshape(head_shape),
            preferred_element_type=jnp.float32,
        ) * (1.0 / math.sqrt(HD))
        scores = jnp.where(allowed[None], scores, -1e30)
        row_max = jnp.max(scores, axis=-1, keepdims=True)
        exp_scores = jnp.exp(scores - row_max)
        totals = jnp.sum(exp_scores, axis=-1)
        weights = exp_scores.astype(jnp.bfloat16)
        attended = jnp.einsum(
            "hqk,khd->qhd",
            weights,
            incoming[:, 2 * part :].reshape(head_shape),
            preferred_element_type=jnp.float32,
        )
        attended = attended / totals.T[:, :, None]
        back = attended.astype(jnp.bfloat16).reshape(seq_count, rows, part)
        returned = lax.all_to_all(back, "seq", 0, 0, tiled=True)
        own_rows = permute(to_token, returned.reshape(slots, part))
        term = jnp.dot(own_rows, w_out[cols], preferred_element_type=jnp.float32)
        partial_value = term if partial_value is None else partial_value + term
    summed = lax.psum_scatter(
        partial_value.astype(jnp.bfloat16), "head", scatter_dimension=1, tiled=True
    )
    return summed


def solution(mesh):
    return jax.shard_map(
        body,
        mesh=mesh,
        in_specs=(
            P("seq", "head"),
            P("seq", "head"),
            P("seq", "head"),
            P("head", "seq", None),
            P("head", None),
        ),
        out_specs=P("seq", "head"),
        check_vma=False,
    )
```

```python
import math

import jax
import jax.numpy as jnp
from jax import lax
from jax.sharding import PartitionSpec as P

HD = 128
NCLUST = 256
CAP = 4
OWNER_CAP = 24
NSPLIT = 2


def attend(queries, keys, values, counts):
    batch, rows_all, features = queries.shape
    heads_here = features // HD
    capacity = rows_all // counts.shape[1]
    head_shape = (batch, rows_all, heads_here, HD)
    scores = jnp.einsum(
        "bqhd,bkhd->bhqk",
        queries.reshape(head_shape),
        keys.reshape(head_shape),
        preferred_element_type=jnp.float32,
    ) * (1.0 / math.sqrt(HD))
    key_order = jnp.arange(rows_all, dtype=jnp.int32)
    filled = jnp.repeat(counts.astype(jnp.float32), capacity, axis=1)
    present = (key_order % capacity).astype(jnp.float32)[None, :] < filled
    causal = key_order[None, :] <= key_order[:, None]
    diagonal_on = key_order[None, :] == key_order[:, None]
    allowed = present[:, None, None, :] & causal[None, None] | diagonal_on[None, None]
    scores = jnp.where(allowed, scores, -1e30)
    row_max = jnp.max(scores, axis=-1, keepdims=True)
    exp_scores = jnp.exp(scores - row_max)
    totals = jnp.sum(exp_scores, axis=-1)
    weights = exp_scores.astype(jnp.bfloat16)
    attended = jnp.einsum(
        "bhqk,bkhd->bqhd", weights, values.reshape(head_shape), preferred_element_type=jnp.float32
    )
    attended = attended / jnp.transpose(totals, (0, 2, 1))[..., None]
    return attended.astype(jnp.bfloat16).reshape(batch, rows_all, features)


def attend_heads(queries, keys, values, counts):
    heads_here, batch, rows_all, _ = queries.shape
    capacity = rows_all // counts.shape[1]
    scores = jnp.einsum(
        "hbqd,hbkd->hbqk", queries, keys, preferred_element_type=jnp.float32
    ) * (1.0 / math.sqrt(HD))
    key_order = jnp.arange(rows_all, dtype=jnp.int32)
    filled = jnp.repeat(counts.astype(jnp.float32), capacity, axis=1)
    present = (key_order % capacity).astype(jnp.float32)[None, :] < filled
    causal = key_order[None, :] <= key_order[:, None]
    diagonal_on = key_order[None, :] == key_order[:, None]
    allowed = present[:, None, :] & causal[None] | diagonal_on[None]
    scores = jnp.where(allowed[None], scores, -1e30)
    row_max = jnp.max(scores, axis=-1, keepdims=True)
    exp_scores = jnp.exp(scores - row_max)
    totals = jnp.sum(exp_scores, axis=-1, keepdims=True)
    weights = exp_scores.astype(jnp.bfloat16)
    attended = jnp.einsum("hbqk,hbkd->hbqd", weights, values, preferred_element_type=jnp.float32)
    attended = attended / totals
    return attended.astype(jnp.bfloat16).reshape(heads_here, batch * rows_all, HD)


def one_hot(index, size):
    return (index[:, None] == jnp.arange(size, dtype=jnp.int32)[None, :]).astype(jnp.bfloat16)


def permute(selector, block):
    return jnp.dot(selector, block, preferred_element_type=jnp.float32).astype(jnp.bfloat16)


def body(queries, keys, values, cluster_ids, w_out):
    cluster = cluster_ids[0, :, 0]
    tokens = cluster.shape[0]
    seq_count = lax.axis_size("seq")
    cl_dev = NCLUST // seq_count
    features = queries.shape[1]
    heads_here = features // HD
    split = NSPLIT if heads_here % NSPLIT == 0 else 1
    part = features // split
    rows = OWNER_CAP
    slots = seq_count * rows
    bucket_rows = cl_dev * seq_count * CAP
    owner = cluster // cl_dev
    position = jnp.arange(tokens, dtype=jnp.int32)

    order_key = cluster * tokens + position
    same_owner = owner[:, None] == owner[None, :]
    before = order_key[None, :] < order_key[:, None]
    rank = jnp.sum((same_owner & before).astype(jnp.int32), axis=1)
    dest = owner * rows + rank
    to_token = one_hot(dest, slots)
    to_slot = to_token.T

    counts = jnp.sum(
        (cluster[:, None] == jnp.arange(NCLUST, dtype=jnp.int32)[None, :]).astype(jnp.int32),
        axis=0,
    ).reshape(seq_count, cl_dev)
    count_in = lax.all_to_all(counts, "seq", 0, 0, tiled=True)

    ends = jnp.cumsum(count_in, axis=1)
    j = jnp.arange(rows, dtype=jnp.int32)
    c_of = jnp.sum((ends[:, None, :] <= j[None, :, None]).astype(jnp.int32), axis=2)
    row_cluster = c_of.reshape(slots)
    valid = row_cluster < cl_dev
    flat = jnp.arange(slots, dtype=jnp.int32)
    allowed = (
        (row_cluster[:, None] == row_cluster[None, :])
        & valid[None, :]
        & (flat[None, :] <= flat[:, None])
    ) | (flat[None, :] == flat[:, None])

    partial_value = None
    for k in range(split):
        cols = slice(k * part, (k + 1) * part)
        packed = jnp.concatenate([queries[:, cols], keys[:, cols], values[:, cols]], axis=1)
        outgoing = permute(to_slot, packed).reshape(seq_count, rows, 3 * part)
        incoming = lax.all_to_all(outgoing, "seq", 0, 0, tiled=True).reshape(slots, 3 * part)
        if k > 0:
            incoming, back = lax.optimization_barrier((incoming, back))
            returned = lax.all_to_all(back, "seq", 0, 0, tiled=True)
            own_rows = permute(to_token, returned.reshape(slots, part))
            term = jnp.dot(own_rows, w_out[prev_cols], preferred_element_type=jnp.float32)
            partial_value = term if partial_value is None else partial_value + term
        heads_part = part // HD
        head_shape = (slots, heads_part, HD)
        scores = jnp.einsum(
            "qhd,khd->hqk",
            incoming[:, :part].reshape(head_shape),
            incoming[:, part : 2 * part].reshape(head_shape),
            preferred_element_type=jnp.float32,
        ) * (1.0 / math.sqrt(HD))
        scores = jnp.where(allowed[None], scores, -1e30)
        row_max = jnp.max(scores, axis=-1, keepdims=True)
        exp_scores = jnp.exp(scores - row_max)
        totals = jnp.sum(exp_scores, axis=-1)
        weights = exp_scores.astype(jnp.bfloat16)
        attended = jnp.einsum(
            "hqk,khd->qhd",
            weights,
            incoming[:, 2 * part :].reshape(head_shape),
            preferred_element_type=jnp.float32,
        )
        attended = attended / totals.T[:, :, None]
        back = attended.astype(jnp.bfloat16).reshape(seq_count, rows, part)
        prev_cols = cols
    returned = lax.all_to_all(back, "seq", 0, 0, tiled=True)
    own_rows = permute(to_token, returned.reshape(slots, part))
    term = jnp.dot(own_rows, w_out[prev_cols], preferred_element_type=jnp.float32)
    partial_value = term if partial_value is None else partial_value + term
    summed = lax.psum_scatter(
        partial_value.astype(jnp.bfloat16), "head", scatter_dimension=1, tiled=True
    )
    return summed


def solution(mesh):
    return jax.shard_map(
        body,
        mesh=mesh,
        in_specs=(
            P("seq", "head"),
            P("seq", "head"),
            P("seq", "head"),
            P("head", "seq", None),
            P("head", None),
        ),
        out_specs=P("seq", "head"),
        check_vma=False,
    )
```

```python
import math

import jax
import jax.numpy as jnp
from jax import lax
from jax.sharding import PartitionSpec as P

HD = 128
NCLUST = 256
CAP = 4
OWNER_CAP = 24
NSPLIT = 2
QCHUNKS = 4


def attend(queries, keys, values, counts):
    batch, rows_all, features = queries.shape
    heads_here = features // HD
    capacity = rows_all // counts.shape[1]
    head_shape = (batch, rows_all, heads_here, HD)
    scores = jnp.einsum(
        "bqhd,bkhd->bhqk",
        queries.reshape(head_shape),
        keys.reshape(head_shape),
        preferred_element_type=jnp.float32,
    ) * (1.0 / math.sqrt(HD))
    key_order = jnp.arange(rows_all, dtype=jnp.int32)
    filled = jnp.repeat(counts.astype(jnp.float32), capacity, axis=1)
    present = (key_order % capacity).astype(jnp.float32)[None, :] < filled
    causal = key_order[None, :] <= key_order[:, None]
    diagonal_on = key_order[None, :] == key_order[:, None]
    allowed = present[:, None, None, :] & causal[None, None] | diagonal_on[None, None]
    scores = jnp.where(allowed, scores, -1e30)
    row_max = jnp.max(scores, axis=-1, keepdims=True)
    exp_scores = jnp.exp(scores - row_max)
    totals = jnp.sum(exp_scores, axis=-1)
    weights = exp_scores.astype(jnp.bfloat16)
    attended = jnp.einsum(
        "bhqk,bkhd->bqhd", weights, values.reshape(head_shape), preferred_element_type=jnp.float32
    )
    attended = attended / jnp.transpose(totals, (0, 2, 1))[..., None]
    return attended.astype(jnp.bfloat16).reshape(batch, rows_all, features)


def attend_heads(queries, keys, values, counts):
    heads_here, batch, rows_all, _ = queries.shape
    capacity = rows_all // counts.shape[1]
    scores = jnp.einsum(
        "hbqd,hbkd->hbqk", queries, keys, preferred_element_type=jnp.float32
    ) * (1.0 / math.sqrt(HD))
    key_order = jnp.arange(rows_all, dtype=jnp.int32)
    filled = jnp.repeat(counts.astype(jnp.float32), capacity, axis=1)
    present = (key_order % capacity).astype(jnp.float32)[None, :] < filled
    causal = key_order[None, :] <= key_order[:, None]
    diagonal_on = key_order[None, :] == key_order[:, None]
    allowed = present[:, None, :] & causal[None] | diagonal_on[None]
    scores = jnp.where(allowed[None], scores, -1e30)
    row_max = jnp.max(scores, axis=-1, keepdims=True)
    exp_scores = jnp.exp(scores - row_max)
    totals = jnp.sum(exp_scores, axis=-1, keepdims=True)
    weights = exp_scores.astype(jnp.bfloat16)
    attended = jnp.einsum("hbqk,hbkd->hbqd", weights, values, preferred_element_type=jnp.float32)
    attended = attended / totals
    return attended.astype(jnp.bfloat16).reshape(heads_here, batch * rows_all, HD)


def one_hot(index, size):
    return (index[:, None] == jnp.arange(size, dtype=jnp.int32)[None, :]).astype(jnp.bfloat16)


def permute(selector, block):
    return jnp.dot(selector, block, preferred_element_type=jnp.float32).astype(jnp.bfloat16)


def body(queries, keys, values, cluster_ids, w_out):
    cluster = cluster_ids[0, :, 0]
    tokens = cluster.shape[0]
    seq_count = lax.axis_size("seq")
    cl_dev = NCLUST // seq_count
    features = queries.shape[1]
    heads_here = features // HD
    split = NSPLIT if heads_here % NSPLIT == 0 else 1
    part = features // split
    rows = OWNER_CAP
    slots = seq_count * rows
    bucket_rows = cl_dev * seq_count * CAP
    owner = cluster // cl_dev
    position = jnp.arange(tokens, dtype=jnp.int32)

    order_key = cluster * tokens + position
    same_owner = owner[:, None] == owner[None, :]
    before = order_key[None, :] < order_key[:, None]
    rank = jnp.sum((same_owner & before).astype(jnp.int32), axis=1)
    dest = owner * rows + rank
    to_token = one_hot(dest, slots)
    to_slot = to_token.T

    counts = jnp.sum(
        (cluster[:, None] == jnp.arange(NCLUST, dtype=jnp.int32)[None, :]).astype(jnp.int32),
        axis=0,
    ).reshape(seq_count, cl_dev)
    count_in = lax.all_to_all(counts, "seq", 0, 0, tiled=True)

    ends = jnp.cumsum(count_in, axis=1)
    j = jnp.arange(rows, dtype=jnp.int32)
    c_of = jnp.sum((ends[:, None, :] <= j[None, :, None]).astype(jnp.int32), axis=2)
    row_cluster = c_of.reshape(slots)
    valid = row_cluster < cl_dev
    flat = jnp.arange(slots, dtype=jnp.int32)
    allowed = (
        (row_cluster[:, None] == row_cluster[None, :])
        & valid[None, :]
        & (flat[None, :] <= flat[:, None])
    ) | (flat[None, :] == flat[:, None])

    partial_value = None
    for k in range(split):
        cols = slice(k * part, (k + 1) * part)
        packed = jnp.concatenate([queries[:, cols], keys[:, cols], values[:, cols]], axis=1)
        outgoing = permute(to_slot, packed).reshape(seq_count, rows, 3 * part)
        incoming = lax.all_to_all(outgoing, "seq", 0, 0, tiled=True).reshape(slots, 3 * part)
        if k > 0:
            incoming, back = lax.optimization_barrier((incoming, back))
            returned = lax.all_to_all(back, "seq", 0, 0, tiled=True)
            own_rows = permute(to_token, returned.reshape(slots, part))
            term = jnp.dot(own_rows, w_out[prev_cols], preferred_element_type=jnp.float32)
            partial_value = term if partial_value is None else partial_value + term
        heads_part = part // HD
        head_shape = (slots, heads_part, HD)
        q_all = incoming[:, :part].reshape(head_shape)
        k_all = incoming[:, part : 2 * part].reshape(head_shape)
        v_all = incoming[:, 2 * part :].reshape(head_shape)
        step = slots // QCHUNKS
        pieces = []
        for i in range(QCHUNKS):
            lo, hi = i * step, (i + 1) * step
            scores = jnp.einsum(
                "qhd,khd->hqk", q_all[lo:hi], k_all[:hi], preferred_element_type=jnp.float32
            ) * (1.0 / math.sqrt(HD))
            scores = jnp.where(allowed[None, lo:hi, :hi], scores, -1e30)
            row_max = jnp.max(scores, axis=-1, keepdims=True)
            exp_scores = jnp.exp(scores - row_max)
            totals = jnp.sum(exp_scores, axis=-1)
            weights = exp_scores.astype(jnp.bfloat16)
            piece = jnp.einsum(
                "hqk,khd->qhd", weights, v_all[:hi], preferred_element_type=jnp.float32
            )
            pieces.append(piece / totals.T[:, :, None])
        attended = jnp.concatenate(pieces, axis=0)
        back = attended.astype(jnp.bfloat16).reshape(seq_count, rows, part)
        prev_cols = cols
    returned = lax.all_to_all(back, "seq", 0, 0, tiled=True)
    own_rows = permute(to_token, returned.reshape(slots, part))
    term = jnp.dot(own_rows, w_out[prev_cols], preferred_element_type=jnp.float32)
    partial_value = term if partial_value is None else partial_value + term
    summed = lax.psum_scatter(
        partial_value.astype(jnp.bfloat16), "head", scatter_dimension=1, tiled=True
    )
    return summed


def solution(mesh):
    return jax.shard_map(
        body,
        mesh=mesh,
        in_specs=(
            P("seq", "head"),
            P("seq", "head"),
            P("seq", "head"),
            P("head", "seq", None),
            P("head", None),
        ),
        out_specs=P("seq", "head"),
        check_vma=False,
    )
```

```python
import math

import jax
import jax.numpy as jnp
from jax import lax
from jax.sharding import PartitionSpec as P

HD = 128
NCLUST = 256
CAP = 4
OWNER_CAP = 24
NSPLIT = 2


def attend(queries, keys, values, counts):
    batch, rows_all, features = queries.shape
    heads_here = features // HD
    capacity = rows_all // counts.shape[1]
    head_shape = (batch, rows_all, heads_here, HD)
    scores = jnp.einsum(
        "bqhd,bkhd->bhqk",
        queries.reshape(head_shape),
        keys.reshape(head_shape),
        preferred_element_type=jnp.float32,
    ) * (1.0 / math.sqrt(HD))
    key_order = jnp.arange(rows_all, dtype=jnp.int32)
    filled = jnp.repeat(counts.astype(jnp.float32), capacity, axis=1)
    present = (key_order % capacity).astype(jnp.float32)[None, :] < filled
    causal = key_order[None, :] <= key_order[:, None]
    diagonal_on = key_order[None, :] == key_order[:, None]
    allowed = present[:, None, None, :] & causal[None, None] | diagonal_on[None, None]
    scores = jnp.where(allowed, scores, -1e30)
    row_max = jnp.max(scores, axis=-1, keepdims=True)
    exp_scores = jnp.exp(scores - row_max)
    totals = jnp.sum(exp_scores, axis=-1)
    weights = exp_scores.astype(jnp.bfloat16)
    attended = jnp.einsum(
        "bhqk,bkhd->bqhd", weights, values.reshape(head_shape), preferred_element_type=jnp.float32
    )
    attended = attended / jnp.transpose(totals, (0, 2, 1))[..., None]
    return attended.astype(jnp.bfloat16).reshape(batch, rows_all, features)


def attend_heads(queries, keys, values, counts):
    heads_here, batch, rows_all, _ = queries.shape
    capacity = rows_all // counts.shape[1]
    scores = jnp.einsum(
        "hbqd,hbkd->hbqk", queries, keys, preferred_element_type=jnp.float32
    ) * (1.0 / math.sqrt(HD))
    key_order = jnp.arange(rows_all, dtype=jnp.int32)
    filled = jnp.repeat(counts.astype(jnp.float32), capacity, axis=1)
    present = (key_order % capacity).astype(jnp.float32)[None, :] < filled
    causal = key_order[None, :] <= key_order[:, None]
    diagonal_on = key_order[None, :] == key_order[:, None]
    allowed = present[:, None, :] & causal[None] | diagonal_on[None]
    scores = jnp.where(allowed[None], scores, -1e30)
    row_max = jnp.max(scores, axis=-1, keepdims=True)
    exp_scores = jnp.exp(scores - row_max)
    totals = jnp.sum(exp_scores, axis=-1, keepdims=True)
    weights = exp_scores.astype(jnp.bfloat16)
    attended = jnp.einsum("hbqk,hbkd->hbqd", weights, values, preferred_element_type=jnp.float32)
    attended = attended / totals
    return attended.astype(jnp.bfloat16).reshape(heads_here, batch * rows_all, HD)


def one_hot(index, size):
    return (index[:, None] == jnp.arange(size, dtype=jnp.int32)[None, :]).astype(jnp.bfloat16)


def permute(selector, block):
    return jnp.dot(selector, block, preferred_element_type=jnp.float32).astype(jnp.bfloat16)


def body(queries, keys, values, cluster_ids, w_out):
    cluster = cluster_ids[0, :, 0]
    tokens = cluster.shape[0]
    seq_count = lax.axis_size("seq")
    cl_dev = NCLUST // seq_count
    features = queries.shape[1]
    heads_here = features // HD
    split = NSPLIT if heads_here % NSPLIT == 0 else 1
    part = features // split
    rows = OWNER_CAP
    slots = seq_count * rows
    bucket_rows = cl_dev * seq_count * CAP
    owner = cluster // cl_dev
    position = jnp.arange(tokens, dtype=jnp.int32)

    order_key = cluster * tokens + position
    same_owner = owner[:, None] == owner[None, :]
    before = order_key[None, :] < order_key[:, None]
    rank = jnp.sum((same_owner & before).astype(jnp.int32), axis=1)
    dest = owner * rows + rank
    to_token = one_hot(dest, slots)
    to_slot = to_token.T

    counts = jnp.sum(
        (cluster[:, None] == jnp.arange(NCLUST, dtype=jnp.int32)[None, :]).astype(jnp.int32),
        axis=0,
    ).reshape(seq_count, cl_dev)
    count_in = lax.all_to_all(counts, "seq", 0, 0, tiled=True)

    ends = jnp.cumsum(count_in, axis=1)
    j = jnp.arange(rows, dtype=jnp.int32)
    c_of = jnp.sum((ends[:, None, :] <= j[None, :, None]).astype(jnp.int32), axis=2)
    row_cluster = c_of.reshape(slots)
    valid = row_cluster < cl_dev
    flat = jnp.arange(slots, dtype=jnp.int32)
    allowed = (
        (row_cluster[:, None] == row_cluster[None, :])
        & valid[None, :]
        & (flat[None, :] <= flat[:, None])
    ) | (flat[None, :] == flat[:, None])

    partial_value = None
    for k in range(split):
        cols = slice(k * part, (k + 1) * part)
        packed = jnp.concatenate([queries[:, cols], keys[:, cols], values[:, cols]], axis=1)
        outgoing = permute(to_slot, packed).reshape(seq_count, rows, 3 * part)
        incoming = lax.all_to_all(outgoing, "seq", 0, 0, tiled=True).reshape(slots, 3 * part)
        if k > 0:
            incoming, back = lax.optimization_barrier((incoming, back))
            returned = lax.all_to_all(back, "seq", 0, 0, tiled=True)
            own_rows = permute(to_token, returned.reshape(slots, part))
            term = jnp.dot(own_rows, w_out[prev_cols], preferred_element_type=jnp.float32)
            partial_value = term if partial_value is None else partial_value + term
        heads_part = part // HD
        head_shape = (slots, heads_part, HD)
        scores = jnp.einsum(
            "qhd,khd->hqk",
            incoming[:, :part].reshape(head_shape),
            incoming[:, part : 2 * part].reshape(head_shape),
            preferred_element_type=jnp.float32,
        ) * (1.0 / math.sqrt(HD))
        scores = jnp.where(allowed[None], scores, -1e30)
        row_max = jnp.max(scores, axis=-1, keepdims=True)
        exp_scores = jnp.exp(scores - row_max)
        totals = jnp.sum(exp_scores, axis=-1)
        weights = exp_scores.astype(jnp.bfloat16)
        attended = jnp.einsum(
            "hqk,khd->qhd",
            weights,
            incoming[:, 2 * part :].reshape(head_shape),
            preferred_element_type=jnp.float32,
        )
        attended = attended / totals.T[:, :, None]
        back = attended.astype(jnp.bfloat16).reshape(seq_count, rows, part)
        prev_cols = cols
    returned = lax.all_to_all(back, "seq", 0, 0, tiled=True)
    own_rows = permute(to_token, returned.reshape(slots, part))
    half = tokens // 2
    outs = []
    for lo in (0, half):
        term = jnp.dot(own_rows[lo : lo + half], w_out[prev_cols], preferred_element_type=jnp.float32)
        if partial_value is not None:
            term = partial_value[lo : lo + half] + term
        outs.append(
            lax.psum_scatter(term.astype(jnp.bfloat16), "head", scatter_dimension=1, tiled=True)
        )
    summed = jnp.concatenate(outs, axis=0)
    return summed


def solution(mesh):
    return jax.shard_map(
        body,
        mesh=mesh,
        in_specs=(
            P("seq", "head"),
            P("seq", "head"),
            P("seq", "head"),
            P("head", "seq", None),
            P("head", None),
        ),
        out_specs=P("seq", "head"),
        check_vma=False,
    )
```

```python
import math

import jax
import jax.numpy as jnp
from jax import lax
from jax.sharding import PartitionSpec as P

HD = 128
NCLUST = 256
CAP = 4
OWNER_CAP = 24
NSPLIT = 2


def attend(queries, keys, values, counts):
    batch, rows_all, features = queries.shape
    heads_here = features // HD
    capacity = rows_all // counts.shape[1]
    head_shape = (batch, rows_all, heads_here, HD)
    scores = jnp.einsum(
        "bqhd,bkhd->bhqk",
        queries.reshape(head_shape),
        keys.reshape(head_shape),
        preferred_element_type=jnp.float32,
    ) * (1.0 / math.sqrt(HD))
    key_order = jnp.arange(rows_all, dtype=jnp.int32)
    filled = jnp.repeat(counts.astype(jnp.float32), capacity, axis=1)
    present = (key_order % capacity).astype(jnp.float32)[None, :] < filled
    causal = key_order[None, :] <= key_order[:, None]
    diagonal_on = key_order[None, :] == key_order[:, None]
    allowed = present[:, None, None, :] & causal[None, None] | diagonal_on[None, None]
    scores = jnp.where(allowed, scores, -1e30)
    row_max = jnp.max(scores, axis=-1, keepdims=True)
    exp_scores = jnp.exp(scores - row_max)
    totals = jnp.sum(exp_scores, axis=-1)
    weights = exp_scores.astype(jnp.bfloat16)
    attended = jnp.einsum(
        "bhqk,bkhd->bqhd", weights, values.reshape(head_shape), preferred_element_type=jnp.float32
    )
    attended = attended / jnp.transpose(totals, (0, 2, 1))[..., None]
    return attended.astype(jnp.bfloat16).reshape(batch, rows_all, features)


def attend_heads(queries, keys, values, counts):
    heads_here, batch, rows_all, _ = queries.shape
    capacity = rows_all // counts.shape[1]
    scores = jnp.einsum(
        "hbqd,hbkd->hbqk", queries, keys, preferred_element_type=jnp.float32
    ) * (1.0 / math.sqrt(HD))
    key_order = jnp.arange(rows_all, dtype=jnp.int32)
    filled = jnp.repeat(counts.astype(jnp.float32), capacity, axis=1)
    present = (key_order % capacity).astype(jnp.float32)[None, :] < filled
    causal = key_order[None, :] <= key_order[:, None]
    diagonal_on = key_order[None, :] == key_order[:, None]
    allowed = present[:, None, :] & causal[None] | diagonal_on[None]
    scores = jnp.where(allowed[None], scores, -1e30)
    row_max = jnp.max(scores, axis=-1, keepdims=True)
    exp_scores = jnp.exp(scores - row_max)
    totals = jnp.sum(exp_scores, axis=-1, keepdims=True)
    weights = exp_scores.astype(jnp.bfloat16)
    attended = jnp.einsum("hbqk,hbkd->hbqd", weights, values, preferred_element_type=jnp.float32)
    attended = attended / totals
    return attended.astype(jnp.bfloat16).reshape(heads_here, batch * rows_all, HD)


def one_hot(index, size):
    return (index[:, None] == jnp.arange(size, dtype=jnp.int32)[None, :]).astype(jnp.bfloat16)


def permute(selector, block):
    return jnp.dot(selector, block, preferred_element_type=jnp.float32).astype(jnp.bfloat16)


def body(queries, keys, values, cluster_ids, w_out):
    cluster = cluster_ids[0, :, 0]
    tokens = cluster.shape[0]
    seq_count = lax.axis_size("seq")
    cl_dev = NCLUST // seq_count
    features = queries.shape[1]
    heads_here = features // HD
    split = NSPLIT if heads_here % NSPLIT == 0 else 1
    part = features // split
    rows = OWNER_CAP
    slots = seq_count * rows
    bucket_rows = cl_dev * seq_count * CAP
    owner = cluster // cl_dev
    position = jnp.arange(tokens, dtype=jnp.int32)

    order_key = cluster * tokens + position
    same_owner = owner[:, None] == owner[None, :]
    before = order_key[None, :] < order_key[:, None]
    rank = jnp.sum((same_owner & before).astype(jnp.int32), axis=1)
    dest = owner * rows + rank
    to_token = one_hot(dest, slots)
    to_slot = to_token.T

    counts = jnp.sum(
        (cluster[:, None] == jnp.arange(NCLUST, dtype=jnp.int32)[None, :]).astype(jnp.int32),
        axis=0,
    ).reshape(seq_count, cl_dev)
    count_in = lax.all_to_all(counts, "seq", 0, 0, tiled=True)

    ends = jnp.cumsum(count_in, axis=1)
    j = jnp.arange(rows, dtype=jnp.int32)
    c_of = jnp.sum((ends[:, None, :] <= j[None, :, None]).astype(jnp.int32), axis=2)
    row_cluster = c_of.reshape(slots)
    valid = row_cluster < cl_dev
    flat = jnp.arange(slots, dtype=jnp.int32)
    allowed = (
        (row_cluster[:, None] == row_cluster[None, :])
        & valid[None, :]
        & (flat[None, :] <= flat[:, None])
    ) | (flat[None, :] == flat[:, None])

    partial_value = None
    for k in range(split):
        cols = slice(k * part, (k + 1) * part)
        packed = jnp.concatenate([queries[:, cols], keys[:, cols], values[:, cols]], axis=1)
        outgoing = permute(to_slot, packed).reshape(seq_count, rows, 3 * part)
        incoming = lax.all_to_all(outgoing, "seq", 0, 0, tiled=True).reshape(slots, 3 * part)
        if k > 0:
            incoming, back = lax.optimization_barrier((incoming, back))
            returned_prev = lax.all_to_all(back, "seq", 0, 0, tiled=True)
            done_cols = prev_cols
        heads_part = part // HD
        head_shape = (slots, heads_part, HD)
        scores = jnp.einsum(
            "qhd,khd->hqk",
            incoming[:, :part].reshape(head_shape),
            incoming[:, part : 2 * part].reshape(head_shape),
            preferred_element_type=jnp.float32,
        ) * (1.0 / math.sqrt(HD))
        scores = jnp.where(allowed[None], scores, -1e30)
        row_max = jnp.max(scores, axis=-1, keepdims=True)
        exp_scores = jnp.exp(scores - row_max)
        totals = jnp.sum(exp_scores, axis=-1)
        weights = exp_scores.astype(jnp.bfloat16)
        attended = jnp.einsum(
            "hqk,khd->qhd",
            weights,
            incoming[:, 2 * part :].reshape(head_shape),
            preferred_element_type=jnp.float32,
        )
        attended = attended / totals.T[:, :, None]
        back = attended.astype(jnp.bfloat16).reshape(seq_count, rows, part)
        if k > 0:
            back, returned_prev = lax.optimization_barrier((back, returned_prev))
            own_rows = permute(to_token, returned_prev.reshape(slots, part))
            term = jnp.dot(own_rows, w_out[done_cols], preferred_element_type=jnp.float32)
            partial_value = term if partial_value is None else partial_value + term
        prev_cols = cols
    returned = lax.all_to_all(back, "seq", 0, 0, tiled=True)
    own_rows = permute(to_token, returned.reshape(slots, part))
    term = jnp.dot(own_rows, w_out[prev_cols], preferred_element_type=jnp.float32)
    partial_value = term if partial_value is None else partial_value + term
    summed = lax.psum_scatter(
        partial_value.astype(jnp.bfloat16), "head", scatter_dimension=1, tiled=True
    )
    return summed


def solution(mesh):
    return jax.shard_map(
        body,
        mesh=mesh,
        in_specs=(
            P("seq", "head"),
            P("seq", "head"),
            P("seq", "head"),
            P("head", "seq", None),
            P("head", None),
        ),
        out_specs=P("seq", "head"),
        check_vma=False,
    )
```

```python
import math

import jax
import jax.numpy as jnp
from jax import lax
from jax.sharding import PartitionSpec as P

HD = 128
NCLUST = 256
CAP = 4
OWNER_CAP = 24
NSPLIT = 2


def attend(queries, keys, values, counts):
    batch, rows_all, features = queries.shape
    heads_here = features // HD
    capacity = rows_all // counts.shape[1]
    head_shape = (batch, rows_all, heads_here, HD)
    scores = jnp.einsum(
        "bqhd,bkhd->bhqk",
        queries.reshape(head_shape),
        keys.reshape(head_shape),
        preferred_element_type=jnp.float32,
    ) * (1.0 / math.sqrt(HD))
    key_order = jnp.arange(rows_all, dtype=jnp.int32)
    filled = jnp.repeat(counts.astype(jnp.float32), capacity, axis=1)
    present = (key_order % capacity).astype(jnp.float32)[None, :] < filled
    causal = key_order[None, :] <= key_order[:, None]
    diagonal_on = key_order[None, :] == key_order[:, None]
    allowed = present[:, None, None, :] & causal[None, None] | diagonal_on[None, None]
    scores = jnp.where(allowed, scores, -1e30)
    row_max = jnp.max(scores, axis=-1, keepdims=True)
    exp_scores = jnp.exp(scores - row_max)
    totals = jnp.sum(exp_scores, axis=-1)
    weights = exp_scores.astype(jnp.bfloat16)
    attended = jnp.einsum(
        "bhqk,bkhd->bqhd", weights, values.reshape(head_shape), preferred_element_type=jnp.float32
    )
    attended = attended / jnp.transpose(totals, (0, 2, 1))[..., None]
    return attended.astype(jnp.bfloat16).reshape(batch, rows_all, features)


def attend_heads(queries, keys, values, counts):
    heads_here, batch, rows_all, _ = queries.shape
    capacity = rows_all // counts.shape[1]
    scores = jnp.einsum(
        "hbqd,hbkd->hbqk", queries, keys, preferred_element_type=jnp.float32
    ) * (1.0 / math.sqrt(HD))
    key_order = jnp.arange(rows_all, dtype=jnp.int32)
    filled = jnp.repeat(counts.astype(jnp.float32), capacity, axis=1)
    present = (key_order % capacity).astype(jnp.float32)[None, :] < filled
    causal = key_order[None, :] <= key_order[:, None]
    diagonal_on = key_order[None, :] == key_order[:, None]
    allowed = present[:, None, :] & causal[None] | diagonal_on[None]
    scores = jnp.where(allowed[None], scores, -1e30)
    row_max = jnp.max(scores, axis=-1, keepdims=True)
    exp_scores = jnp.exp(scores - row_max)
    totals = jnp.sum(exp_scores, axis=-1, keepdims=True)
    weights = exp_scores.astype(jnp.bfloat16)
    attended = jnp.einsum("hbqk,hbkd->hbqd", weights, values, preferred_element_type=jnp.float32)
    attended = attended / totals
    return attended.astype(jnp.bfloat16).reshape(heads_here, batch * rows_all, HD)


def one_hot(index, size):
    return (index[:, None] == jnp.arange(size, dtype=jnp.int32)[None, :]).astype(jnp.bfloat16)


def permute(selector, block):
    return jnp.dot(selector, block, preferred_element_type=jnp.float32).astype(jnp.bfloat16)


def body(queries, keys, values, cluster_ids, w_out):
    cluster = cluster_ids[0, :, 0]
    tokens = cluster.shape[0]
    seq_count = lax.axis_size("seq")
    cl_dev = NCLUST // seq_count
    features = queries.shape[1]
    heads_here = features // HD
    split = NSPLIT if heads_here % NSPLIT == 0 else 1
    part = features // split
    rows = OWNER_CAP
    slots = seq_count * rows
    bucket_rows = cl_dev * seq_count * CAP
    owner = cluster // cl_dev
    position = jnp.arange(tokens, dtype=jnp.int32)

    order_key = cluster * tokens + position
    same_owner = owner[:, None] == owner[None, :]
    before = order_key[None, :] < order_key[:, None]
    rank = jnp.sum((same_owner & before).astype(jnp.int32), axis=1)
    dest = owner * rows + rank
    to_token = one_hot(dest, slots)
    to_slot = to_token.T

    counts = jnp.sum(
        (cluster[:, None] == jnp.arange(NCLUST, dtype=jnp.int32)[None, :]).astype(jnp.int32),
        axis=0,
    ).reshape(seq_count, cl_dev)
    count_in = lax.all_to_all(counts, "seq", 0, 0, tiled=True)

    ends = jnp.cumsum(count_in, axis=1)
    j = jnp.arange(rows, dtype=jnp.int32)
    c_of = jnp.sum((ends[:, None, :] <= j[None, :, None]).astype(jnp.int32), axis=2)
    row_cluster = c_of.reshape(slots)
    valid = row_cluster < cl_dev
    flat = jnp.arange(slots, dtype=jnp.int32)
    allowed = (
        (row_cluster[:, None] == row_cluster[None, :])
        & valid[None, :]
        & (flat[None, :] <= flat[:, None])
    ) | (flat[None, :] == flat[:, None])

    partial_value = None
    for k in range(split):
        cols = slice(k * part, (k + 1) * part)
        packed = jnp.concatenate([queries[:, cols], keys[:, cols], values[:, cols]], axis=1)
        outgoing = permute(to_slot, packed).reshape(seq_count, rows, 3 * part)
        incoming = lax.all_to_all(outgoing, "seq", 0, 0, tiled=True).reshape(slots, 3 * part)
        if k > 0:
            incoming, back = lax.optimization_barrier((incoming, back))
            returned_prev = lax.all_to_all(back, "seq", 0, 0, tiled=True)
            done_cols = prev_cols
        heads_part = part // HD
        head_shape = (slots, heads_part, HD)
        scores = jnp.einsum(
            "qhd,khd->hqk",
            incoming[:, :part].reshape(head_shape),
            incoming[:, part : 2 * part].reshape(head_shape),
            preferred_element_type=jnp.float32,
        ) * (1.0 / math.sqrt(HD))
        scores = jnp.where(allowed[None], scores, -1e30)
        row_max = jnp.max(scores, axis=-1, keepdims=True)
        exp_scores = jnp.exp(scores - row_max)
        totals = jnp.sum(exp_scores, axis=-1)
        weights = exp_scores.astype(jnp.bfloat16)
        attended = jnp.einsum(
            "hqk,khd->qhd",
            weights,
            incoming[:, 2 * part :].reshape(head_shape),
            preferred_element_type=jnp.float32,
        )
        attended = attended / totals.T[:, :, None]
        back = attended.astype(jnp.bfloat16).reshape(seq_count, rows, part)
        if k > 0:
            back, returned_prev = lax.optimization_barrier((back, returned_prev))
            own_rows = permute(to_token, returned_prev.reshape(slots, part))
            term = jnp.dot(own_rows, w_out[done_cols], preferred_element_type=jnp.float32)
            partial_value = term if partial_value is None else partial_value + term
        prev_cols = cols
    returned = lax.all_to_all(back, "seq", 0, 0, tiled=True)
    if partial_value is not None:
        returned, partial_value = lax.optimization_barrier((returned, partial_value))
    own_rows = permute(to_token, returned.reshape(slots, part))
    term = jnp.dot(own_rows, w_out[prev_cols], preferred_element_type=jnp.float32)
    partial_value = term if partial_value is None else partial_value + term
    summed = lax.psum_scatter(
        partial_value.astype(jnp.bfloat16), "head", scatter_dimension=1, tiled=True
    )
    return summed


def solution(mesh):
    return jax.shard_map(
        body,
        mesh=mesh,
        in_specs=(
            P("seq", "head"),
            P("seq", "head"),
            P("seq", "head"),
            P("head", "seq", None),
            P("head", None),
        ),
        out_specs=P("seq", "head"),
        check_vma=False,
    )
```

```python
import math

import jax
import jax.numpy as jnp
from jax import lax
from jax.sharding import PartitionSpec as P

HD = 128
NCLUST = 256
CAP = 4
OWNER_CAP = 24
NSPLIT = 2


def attend(queries, keys, values, counts):
    batch, rows_all, features = queries.shape
    heads_here = features // HD
    capacity = rows_all // counts.shape[1]
    head_shape = (batch, rows_all, heads_here, HD)
    scores = jnp.einsum(
        "bqhd,bkhd->bhqk",
        queries.reshape(head_shape),
        keys.reshape(head_shape),
        preferred_element_type=jnp.float32,
    ) * (1.0 / math.sqrt(HD))
    key_order = jnp.arange(rows_all, dtype=jnp.int32)
    filled = jnp.repeat(counts.astype(jnp.float32), capacity, axis=1)
    present = (key_order % capacity).astype(jnp.float32)[None, :] < filled
    causal = key_order[None, :] <= key_order[:, None]
    diagonal_on = key_order[None, :] == key_order[:, None]
    allowed = present[:, None, None, :] & causal[None, None] | diagonal_on[None, None]
    scores = jnp.where(allowed, scores, -1e30)
    row_max = jnp.max(scores, axis=-1, keepdims=True)
    exp_scores = jnp.exp(scores - row_max)
    totals = jnp.sum(exp_scores, axis=-1)
    weights = exp_scores.astype(jnp.bfloat16)
    attended = jnp.einsum(
        "bhqk,bkhd->bqhd", weights, values.reshape(head_shape), preferred_element_type=jnp.float32
    )
    attended = attended / jnp.transpose(totals, (0, 2, 1))[..., None]
    return attended.astype(jnp.bfloat16).reshape(batch, rows_all, features)


def attend_heads(queries, keys, values, counts):
    heads_here, batch, rows_all, _ = queries.shape
    capacity = rows_all // counts.shape[1]
    scores = jnp.einsum(
        "hbqd,hbkd->hbqk", queries, keys, preferred_element_type=jnp.float32
    ) * (1.0 / math.sqrt(HD))
    key_order = jnp.arange(rows_all, dtype=jnp.int32)
    filled = jnp.repeat(counts.astype(jnp.float32), capacity, axis=1)
    present = (key_order % capacity).astype(jnp.float32)[None, :] < filled
    causal = key_order[None, :] <= key_order[:, None]
    diagonal_on = key_order[None, :] == key_order[:, None]
    allowed = present[:, None, :] & causal[None] | diagonal_on[None]
    scores = jnp.where(allowed[None], scores, -1e30)
    row_max = jnp.max(scores, axis=-1, keepdims=True)
    exp_scores = jnp.exp(scores - row_max)
    totals = jnp.sum(exp_scores, axis=-1, keepdims=True)
    weights = exp_scores.astype(jnp.bfloat16)
    attended = jnp.einsum("hbqk,hbkd->hbqd", weights, values, preferred_element_type=jnp.float32)
    attended = attended / totals
    return attended.astype(jnp.bfloat16).reshape(heads_here, batch * rows_all, HD)


def one_hot(index, size):
    return (index[:, None] == jnp.arange(size, dtype=jnp.int32)[None, :]).astype(jnp.bfloat16)


def permute(selector, block):
    return jnp.dot(selector, block, preferred_element_type=jnp.float32).astype(jnp.bfloat16)


def body(queries, keys, values, cluster_ids, w_out):
    cluster = cluster_ids[0, :, 0]
    tokens = cluster.shape[0]
    seq_count = lax.axis_size("seq")
    cl_dev = NCLUST // seq_count
    features = queries.shape[1]
    heads_here = features // HD
    split = NSPLIT if heads_here % NSPLIT == 0 else 1
    part = features // split
    rows = OWNER_CAP
    slots = seq_count * rows
    bucket_rows = cl_dev * seq_count * CAP
    owner = cluster // cl_dev
    position = jnp.arange(tokens, dtype=jnp.int32)

    order_key = cluster * tokens + position
    same_owner = owner[:, None] == owner[None, :]
    before = order_key[None, :] < order_key[:, None]
    rank = jnp.sum((same_owner & before).astype(jnp.int32), axis=1)
    dest = owner * rows + rank
    to_token = one_hot(dest, slots)
    to_slot = to_token.T

    tag = jnp.zeros((tokens, HD), jnp.bfloat16).at[:, 0].set(
        (cluster % cl_dev + 1).astype(jnp.bfloat16)
    )

    flat = jnp.arange(slots, dtype=jnp.int32)

    partial_value = None
    for k in range(split):
        cols = slice(k * part, (k + 1) * part)
        pieces = [queries[:, cols], keys[:, cols], values[:, cols]] + ([tag] if k == 0 else [])
        packed = jnp.concatenate(pieces, axis=1)
        width = packed.shape[1]
        outgoing = permute(to_slot, packed).reshape(seq_count, rows, width)
        incoming = lax.all_to_all(outgoing, "seq", 0, 0, tiled=True).reshape(slots, width)
        if k == 0:
            row_cluster = incoming[:, 3 * part].astype(jnp.int32) - 1
            valid = row_cluster >= 0
            allowed = (
                (row_cluster[:, None] == row_cluster[None, :])
                & valid[None, :]
                & (flat[None, :] <= flat[:, None])
            ) | (flat[None, :] == flat[:, None])
        if k > 0:
            incoming, back = lax.optimization_barrier((incoming, back))
            returned_prev = lax.all_to_all(back, "seq", 0, 0, tiled=True)
            done_cols = prev_cols
        heads_part = part // HD
        head_shape = (slots, heads_part, HD)
        scores = jnp.einsum(
            "qhd,khd->hqk",
            incoming[:, :part].reshape(head_shape),
            incoming[:, part : 2 * part].reshape(head_shape),
            preferred_element_type=jnp.float32,
        ) * (1.0 / math.sqrt(HD))
        scores = jnp.where(allowed[None], scores, -1e30)
        row_max = jnp.max(scores, axis=-1, keepdims=True)
        exp_scores = jnp.exp(scores - row_max)
        totals = jnp.sum(exp_scores, axis=-1)
        weights = exp_scores.astype(jnp.bfloat16)
        attended = jnp.einsum(
            "hqk,khd->qhd",
            weights,
            incoming[:, 2 * part : 3 * part].reshape(head_shape),
            preferred_element_type=jnp.float32,
        )
        attended = attended / totals.T[:, :, None]
        back = attended.astype(jnp.bfloat16).reshape(seq_count, rows, part)
        if k > 0:
            back, returned_prev = lax.optimization_barrier((back, returned_prev))
            own_rows = permute(to_token, returned_prev.reshape(slots, part))
            term = jnp.dot(own_rows, w_out[done_cols], preferred_element_type=jnp.float32)
            partial_value = term if partial_value is None else partial_value + term
        prev_cols = cols
    returned = lax.all_to_all(back, "seq", 0, 0, tiled=True)
    if partial_value is not None:
        returned, partial_value = lax.optimization_barrier((returned, partial_value))
    own_rows = permute(to_token, returned.reshape(slots, part))
    term = jnp.dot(own_rows, w_out[prev_cols], preferred_element_type=jnp.float32)
    partial_value = term if partial_value is None else partial_value + term
    summed = lax.psum_scatter(
        partial_value.astype(jnp.bfloat16), "head", scatter_dimension=1, tiled=True
    )
    return summed


def solution(mesh):
    return jax.shard_map(
        body,
        mesh=mesh,
        in_specs=(
            P("seq", "head"),
            P("seq", "head"),
            P("seq", "head"),
            P("head", "seq", None),
            P("head", None),
        ),
        out_specs=P("seq", "head"),
        check_vma=False,
    )
```

```python
import math

import jax
import jax.numpy as jnp
from jax import lax
from jax.sharding import PartitionSpec as P

HD = 128
NCLUST = 256
CAP = 4
OWNER_CAP = 24
NSPLIT = 2


def attend(queries, keys, values, counts):
    batch, rows_all, features = queries.shape
    heads_here = features // HD
    capacity = rows_all // counts.shape[1]
    head_shape = (batch, rows_all, heads_here, HD)
    scores = jnp.einsum(
        "bqhd,bkhd->bhqk",
        queries.reshape(head_shape),
        keys.reshape(head_shape),
        preferred_element_type=jnp.float32,
    ) * (1.0 / math.sqrt(HD))
    key_order = jnp.arange(rows_all, dtype=jnp.int32)
    filled = jnp.repeat(counts.astype(jnp.float32), capacity, axis=1)
    present = (key_order % capacity).astype(jnp.float32)[None, :] < filled
    causal = key_order[None, :] <= key_order[:, None]
    diagonal_on = key_order[None, :] == key_order[:, None]
    allowed = present[:, None, None, :] & causal[None, None] | diagonal_on[None, None]
    scores = jnp.where(allowed, scores, -1e30)
    row_max = jnp.max(scores, axis=-1, keepdims=True)
    exp_scores = jnp.exp(scores - row_max)
    totals = jnp.sum(exp_scores, axis=-1)
    weights = exp_scores.astype(jnp.bfloat16)
    attended = jnp.einsum(
        "bhqk,bkhd->bqhd", weights, values.reshape(head_shape), preferred_element_type=jnp.float32
    )
    attended = attended / jnp.transpose(totals, (0, 2, 1))[..., None]
    return attended.astype(jnp.bfloat16).reshape(batch, rows_all, features)


def attend_heads(queries, keys, values, counts):
    heads_here, batch, rows_all, _ = queries.shape
    capacity = rows_all // counts.shape[1]
    scores = jnp.einsum(
        "hbqd,hbkd->hbqk", queries, keys, preferred_element_type=jnp.float32
    ) * (1.0 / math.sqrt(HD))
    key_order = jnp.arange(rows_all, dtype=jnp.int32)
    filled = jnp.repeat(counts.astype(jnp.float32), capacity, axis=1)
    present = (key_order % capacity).astype(jnp.float32)[None, :] < filled
    causal = key_order[None, :] <= key_order[:, None]
    diagonal_on = key_order[None, :] == key_order[:, None]
    allowed = present[:, None, :] & causal[None] | diagonal_on[None]
    scores = jnp.where(allowed[None], scores, -1e30)
    row_max = jnp.max(scores, axis=-1, keepdims=True)
    exp_scores = jnp.exp(scores - row_max)
    totals = jnp.sum(exp_scores, axis=-1, keepdims=True)
    weights = exp_scores.astype(jnp.bfloat16)
    attended = jnp.einsum("hbqk,hbkd->hbqd", weights, values, preferred_element_type=jnp.float32)
    attended = attended / totals
    return attended.astype(jnp.bfloat16).reshape(heads_here, batch * rows_all, HD)


def one_hot(index, size):
    return (index[:, None] == jnp.arange(size, dtype=jnp.int32)[None, :]).astype(jnp.bfloat16)


def permute(selector, block):
    return jnp.dot(selector, block, preferred_element_type=jnp.float32).astype(jnp.bfloat16)


def body(queries, keys, values, cluster_ids, w_out):
    cluster = cluster_ids[0, :, 0]
    tokens = cluster.shape[0]
    seq_count = lax.axis_size("seq")
    cl_dev = NCLUST // seq_count
    features = queries.shape[1]
    heads_here = features // HD
    split = NSPLIT if heads_here % NSPLIT == 0 else 1
    if split == 2 and heads_here % 3 == 0:
        bounds = [0, 2 * features // 3, features]
    else:
        bounds = [k * (features // split) for k in range(split + 1)]
    rows = OWNER_CAP
    slots = seq_count * rows
    bucket_rows = cl_dev * seq_count * CAP
    owner = cluster // cl_dev
    position = jnp.arange(tokens, dtype=jnp.int32)

    order_key = cluster * tokens + position
    same_owner = owner[:, None] == owner[None, :]
    before = order_key[None, :] < order_key[:, None]
    rank = jnp.sum((same_owner & before).astype(jnp.int32), axis=1)
    dest = owner * rows + rank
    to_token = one_hot(dest, slots)
    to_slot = to_token.T

    tag = jnp.zeros((tokens, HD), jnp.bfloat16).at[:, 0].set(
        (cluster % cl_dev + 1).astype(jnp.bfloat16)
    )

    flat = jnp.arange(slots, dtype=jnp.int32)

    partial_value = None
    for k in range(split):
        part = bounds[k + 1] - bounds[k]
        cols = slice(bounds[k], bounds[k + 1])
        pieces = [queries[:, cols], keys[:, cols], values[:, cols]] + ([tag] if k == 0 else [])
        packed = jnp.concatenate(pieces, axis=1)
        width = packed.shape[1]
        outgoing = permute(to_slot, packed).reshape(seq_count, rows, width)
        incoming = lax.all_to_all(outgoing, "seq", 0, 0, tiled=True).reshape(slots, width)
        if k == 0:
            row_cluster = incoming[:, 3 * part].astype(jnp.int32) - 1
            valid = row_cluster >= 0
            allowed = (
                (row_cluster[:, None] == row_cluster[None, :])
                & valid[None, :]
                & (flat[None, :] <= flat[:, None])
            ) | (flat[None, :] == flat[:, None])
        if k > 0:
            incoming, back = lax.optimization_barrier((incoming, back))
            returned_prev = lax.all_to_all(back, "seq", 0, 0, tiled=True)
            done_cols = prev_cols
        heads_part = part // HD
        head_shape = (slots, heads_part, HD)
        scores = jnp.einsum(
            "qhd,khd->hqk",
            incoming[:, :part].reshape(head_shape),
            incoming[:, part : 2 * part].reshape(head_shape),
            preferred_element_type=jnp.float32,
        ) * (1.0 / math.sqrt(HD))
        scores = jnp.where(allowed[None], scores, -1e30)
        row_max = jnp.max(scores, axis=-1, keepdims=True)
        exp_scores = jnp.exp(scores - row_max)
        totals = jnp.sum(exp_scores, axis=-1)
        weights = exp_scores.astype(jnp.bfloat16)
        attended = jnp.einsum(
            "hqk,khd->qhd",
            weights,
            incoming[:, 2 * part : 3 * part].reshape(head_shape),
            preferred_element_type=jnp.float32,
        )
        attended = attended / totals.T[:, :, None]
        back = attended.astype(jnp.bfloat16).reshape(seq_count, rows, part)
        if k > 0:
            back, returned_prev = lax.optimization_barrier((back, returned_prev))
            own_rows = permute(to_token, returned_prev.reshape(slots, -1))
            term = jnp.dot(own_rows, w_out[done_cols], preferred_element_type=jnp.float32)
            partial_value = term if partial_value is None else partial_value + term
        prev_cols = cols
    returned = lax.all_to_all(back, "seq", 0, 0, tiled=True)
    if partial_value is not None:
        returned, partial_value = lax.optimization_barrier((returned, partial_value))
    own_rows = permute(to_token, returned.reshape(slots, -1))
    term = jnp.dot(own_rows, w_out[prev_cols], preferred_element_type=jnp.float32)
    partial_value = term if partial_value is None else partial_value + term
    summed = lax.psum_scatter(
        partial_value.astype(jnp.bfloat16), "head", scatter_dimension=1, tiled=True
    )
    return summed


def solution(mesh):
    return jax.shard_map(
        body,
        mesh=mesh,
        in_specs=(
            P("seq", "head"),
            P("seq", "head"),
            P("seq", "head"),
            P("head", "seq", None),
            P("head", None),
        ),
        out_specs=P("seq", "head"),
        check_vma=False,
    )
```
